128 devices in a mesh: slab: 16 (over x, z_lo, core), sub: 8 (over z_hi, y).
Axes of the slice: x: 4, y: 4, z: 4 (z_hi: 2, z_lo: 2; z = z_hi * 2 + z_lo), core: 2. Of those that a mesh axis runs over, the one named last changes fastest.
Arguments:
- feats: bfloat16 [655360, 128], P(('slab', 'sub')), may hold values from -6 to 6
- coords: bfloat16 [3, 655360], P(None, ('slab', 'sub')), may hold values from 0 to 1, as said below
- serial: int32 [655360], P(('slab', 'sub')), may hold values from 0 to 5119, as said below
- cells: int32 [655360], P(('slab', 'sub')), may hold values from 0 to 262143, as said below
- counts: int32 [128], P(('slab', 'sub')), may hold values from 2 to 5, as said below
- ghosts: int32 [640], P(('slab', 'sub')), may hold values from 0 to 4
- ln1_gain: float32 [128], replicated, may hold values from 0.5 to 1.5
- w_qkv: bfloat16 [128, 384], replicated
- pos_proj: float32 [3, 256], replicated, may hold values from -6 to 6
- w_out: bfloat16 [128, 128], replicated, may hold values from -0.5 to 0.5
- ln2_gain: float32 [128], replicated, may hold values from 0.5 to 1.5
- w_up: bfloat16 [128, 512], replicated, may hold values from -0.5 to 0.5
- w_down: bfloat16 [512, 128], replicated, may hold values from -0.25 to 0.25
Outputs:
- block_out: bfloat16 [655360, 128], P(('slab', 'sub'))
- pooled: float32 [64, 64, 64, 128], P('slab', 'sub')
The draws below stay inside these ranges and needn't reach their ends.
Inputs may be any that keep to these rules, and one draw needn't show every extreme that they name: `counts`: each device block's number of live patch slots; live slots are the lowest ones. Some block holds 5 and some holds 2. `serial`: within each device block, a permutation of its local rows 0 to 5119 whose first counts[b] * 1024 entries are rows below counts[b] * 1024. `cells`: A particle of block s * 8 + t lies in a cell with x in s * 4 to (s + 1) * 4 - 1 and y in t * 8 to (t + 1) * 8 - 1. `coords`: positions lie inside their particle's cell, in box units.
All inputs are finite; a program needn't handle non-finite values.
Results may differ from the reference program's by a relative error of at most 0.01.
The reference program's roundings to bfloat16 on the way count: a program that leaves them out, or rounds other values in their place, can miss the bound.
Values may be sent and summed in bfloat16 or wider, within the bound.
No kernel may reach another device: no remote copies, remote signals or barrier semaphores. Data moves between devices by JAX's collectives and lax.ppermute only.
A program may use at most 128 MiB of HBM per device.

```python
import math
import jax
import jax.numpy as jnp
from jax import lax

WIDTH = 128
HEADS = 4
MLP_UNITS = 512
PATCH = 1024
SLOTS = 5
GRID = 64
SLABS = 16
SUBS = 8
BLOCKS = 128
ROWS = 655360
XPLANES = 4
YROWS = 8


def make_counts(key):
    anchor = jax.random.fold_in(key, 101)
    level = jax.random.randint(jax.random.fold_in(anchor, 1), (BLOCKS,), 0, 5)
    loads = 2 + (SLOTS - 2) * level * level // 16
    busiest = jax.random.randint(jax.random.fold_in(anchor, 2), (), 0, BLOCKS)
    lightest = (busiest + 1 + jax.random.randint(jax.random.fold_in(anchor, 3), (), 0, BLOCKS - 1)) % BLOCKS
    block_ids = jnp.arange(BLOCKS)
    loads = jnp.where(block_ids == lightest, 2, loads)
    loads = jnp.where(block_ids == busiest, SLOTS, loads)
    return loads.astype(jnp.int32)


def cell_parts(key):
    anchor = jax.random.fold_in(key, 303)
    rows_dev = SLOTS * PATCH
    block_no = jnp.arange(ROWS) // rows_dev
    slab_no = block_no // SUBS
    sub_no = block_no % SUBS
    local_x = jax.random.randint(jax.random.fold_in(anchor, 1), (ROWS,), 0, XPLANES)
    local_y = jax.random.randint(jax.random.fold_in(anchor, 2), (ROWS,), 0, YROWS)
    cell_z = jax.random.randint(jax.random.fold_in(anchor, 3), (ROWS,), 0, GRID)
    row_ids = jnp.arange(ROWS)
    lowest = row_ids == 0
    highest = row_ids == (BLOCKS - 1) * rows_dev
    local_x = jnp.where(lowest, 0, jnp.where(highest, XPLANES - 1, local_x))
    local_y = jnp.where(lowest, 0, jnp.where(highest, YROWS - 1, local_y))
    cell_z = jnp.where(lowest, 0, jnp.where(highest, GRID - 1, cell_z))
    return (slab_no * XPLANES + local_x, sub_no * YROWS + local_y, cell_z)


def draw_counts(key, part):
    return make_counts(key)


def draw_serial(key, part):
    loads = make_counts(key)
    rows_dev = SLOTS * PATCH
    noise = jax.random.randint(jax.random.fold_in(key, 202), (BLOCKS, rows_dev), 0, 1024)
    row_ids = jnp.arange(rows_dev)[None, :]
    live = row_ids < loads[:, None] * PATCH
    score = noise * rows_dev + row_ids + jnp.where(live, 0, 1024 * rows_dev)
    return jnp.argsort(score, axis=1, stable=True).astype(jnp.int32).reshape(ROWS)


def draw_cells(key, part):
    cell_x, cell_y, cell_z = cell_parts(key)
    return ((cell_x * GRID + cell_y) * GRID + cell_z).astype(jnp.int32)


def draw_coords(key, part):
    cell_x, cell_y, cell_z = cell_parts(key)
    corner = jnp.stack([cell_x, cell_y, cell_z]).astype(jnp.float32)
    inside = jax.random.uniform(jax.random.fold_in(key, 304), (3, ROWS), jnp.float32, 0.0, 0.999)
    return ((corner + inside) / GRID).astype(jnp.bfloat16)


def draw_w_qkv(key, part):
    anchor = jax.random.normal(jax.random.fold_in(key, 404), (WIDTH, 3 * WIDTH), jnp.float32) * WIDTH ** (-0.5)
    return anchor.astype(jnp.bfloat16)


def place_ends(drawn, rng, low, largest):
    extent = drawn.shape
    spot = [jax.random.randint(jax.random.fold_in(rng, axis), (), 0, extent[axis]) for axis in range(len(extent))]
    drawn = drawn.at[tuple(spot)].set(low)
    longest = extent.index(max(extent))
    spot[longest] = (spot[longest] + 1) % extent[longest]
    return drawn.at[tuple(spot)].set(largest)


def shard_levels(stream_key, dims, shards, smallest, top_value):
    level = 1.0
    for position, parts in shards:
        steps = jax.random.uniform(jax.random.fold_in(jax.random.fold_in(stream_key, 6), position), (parts,), jnp.float32, smallest / len(shards), top_value / len(shards))
        level = level * jnp.repeat(jnp.exp(steps), dims[position] // parts).reshape((-1,) + (1,) * (len(dims) - 1 - position))
    return level


def normal_values(key, extent, scale, reach, cuts=(), kind=jnp.bfloat16):
    values = scale * jax.random.normal(key, extent, jnp.float32)
    if cuts:
        values = values * shard_levels(key, extent, cuts, -0.22, 0.18)
    return jnp.clip(values, -reach, reach).astype(kind)


def setup_inputs(seed: int = 0) -> dict:
    arg_keys = jax.random.split(jax.random.key(seed), 14)
    feats = normal_values(arg_keys[0], (ROWS, WIDTH), 1.0, 6.0, ((0, 128),))
    coords = draw_coords(jax.random.fold_in(arg_keys[13], 71), 0)
    serial = draw_serial(jax.random.fold_in(arg_keys[13], 71), 0)
    cells = draw_cells(jax.random.fold_in(arg_keys[13], 71), 0)
    counts = draw_counts(jax.random.fold_in(arg_keys[13], 71), 0)
    ghosts = place_ends(jax.random.randint(arg_keys[5], (BLOCKS * SLOTS,), 0, 5), jax.random.fold_in(arg_keys[5], 1), 0, 4).astype(jnp.int32)
    ln1_gain = jnp.clip(1.0 + 0.1 * jax.random.normal(arg_keys[6], (WIDTH,), jnp.float32), 0.5, 1.5)
    w_qkv = draw_w_qkv(jax.random.fold_in(arg_keys[13], 71), 0)
    pos_proj = normal_values(arg_keys[8], (3, 2 * WIDTH), 1.0, 6.0, (), jnp.float32)
    w_out = normal_values(arg_keys[9], (WIDTH, WIDTH), WIDTH ** -0.5, 0.5)
    ln2_gain = jnp.clip(1.0 + 0.1 * jax.random.normal(arg_keys[10], (WIDTH,), jnp.float32), 0.5, 1.5)
    w_up = normal_values(arg_keys[11], (WIDTH, MLP_UNITS), WIDTH ** -0.5, 0.5)
    w_down = normal_values(arg_keys[12], (MLP_UNITS, WIDTH), MLP_UNITS ** -0.5, 0.25)
    return dict(feats=feats, coords=coords, serial=serial, cells=cells, counts=counts, ghosts=ghosts, ln1_gain=ln1_gain, w_qkv=w_qkv, pos_proj=pos_proj, w_out=w_out, ln2_gain=ln2_gain, w_up=w_up, w_down=w_down)


eps = 1e-05

def normalize(row_block, gain):
    values = row_block.astype(jnp.float32)
    center = values - lax.optimization_barrier(jnp.mean(values, axis=-1, keepdims=True))
    spread = lax.optimization_barrier(jnp.mean(center * center, axis=-1, keepdims=True))
    return center * lax.rsqrt(spread + eps) * gain

def position_term(place_block, table):
    first = place_block[0][:, None] * table[0][None, :]
    second = place_block[1][:, None] * table[1][None, :]
    third = place_block[2][:, None] * table[2][None, :]
    return first + second + third

def shifted(place_block, axis_number, amount):
    bump = (jnp.arange(3) == axis_number).astype(jnp.float32) * amount
    return place_block + bump[:, None]

def ghost_pair(row_block, place_block, ln1_gain, w_qkv, pos_proj, width):
    normed = normalize(row_block, ln1_gain).astype(jnp.bfloat16)
    qkv_base = jnp.dot(normed, w_qkv[:, width:], preferred_element_type=jnp.float32)
    key_rows = (qkv_base[:, :width] + position_term(place_block, pos_proj[:, width:])).astype(jnp.bfloat16)
    return (key_rows, qkv_base[:, width:].astype(jnp.bfloat16))

def attend(query_rows, key_rows, value_rows, ghost_keys, ghost_values, present):
    points, width = query_rows.shape
    depth = width // HEADS
    scale = 1.0 / math.sqrt(depth)
    query_f = query_rows.reshape(points, HEADS, depth).astype(jnp.float32)
    own_scores = jnp.einsum('phd,khd->hpk', query_f, key_rows.reshape(points, HEADS, depth).astype(jnp.float32)) * scale
    far_scores = jnp.einsum('phd,khd->hpk', query_f, ghost_keys.reshape(points, HEADS, depth).astype(jnp.float32)) * scale
    own_top = lax.optimization_barrier(jnp.max(own_scores, axis=-1))
    highest = jnp.maximum(own_top, jnp.where(present > 0, lax.optimization_barrier(jnp.max(far_scores, axis=-1)), own_top))
    own_exp = jnp.exp(own_scores - highest[..., None])
    far_exp = jnp.where(present > 0, jnp.exp(far_scores - highest[..., None]), 0.0)
    total = lax.optimization_barrier(jnp.sum(own_exp, axis=-1)) + lax.optimization_barrier(jnp.sum(far_exp, axis=-1))
    own_weights = (own_exp / total[..., None]).astype(jnp.bfloat16)
    far_weights = (far_exp / total[..., None]).astype(jnp.bfloat16)
    mixed = jnp.einsum('hpk,khd->phd', own_weights.astype(jnp.float32), value_rows.reshape(points, HEADS, depth).astype(jnp.float32))
    mixed = mixed + jnp.einsum('hpk,khd->phd', far_weights.astype(jnp.float32), ghost_values.reshape(points, HEADS, depth).astype(jnp.float32))
    return mixed.reshape(points, width).astype(jnp.bfloat16)

def finish(ordered_patch, attended, w_out, ln2_gain, w_up, w_down):
    stream = (ordered_patch.astype(jnp.float32) + jnp.dot(attended, w_out, preferred_element_type=jnp.float32)).astype(jnp.bfloat16)
    normed2 = normalize(stream, ln2_gain).astype(jnp.bfloat16)
    inner = jax.nn.gelu(jnp.dot(normed2, w_up, preferred_element_type=jnp.float32)).astype(jnp.bfloat16)
    return (stream.astype(jnp.float32) + jnp.dot(inner, w_down, preferred_element_type=jnp.float32)).astype(jnp.bfloat16)

def reference(feats, coords, serial, cells, counts, ghosts, ln1_gain, w_qkv, pos_proj, w_out, ln2_gain, w_up, w_down):
    rows_dev = SLOTS * PATCH
    serial_blocks = serial.reshape(BLOCKS, rows_dev)
    ordered = jnp.take_along_axis(feats.reshape(BLOCKS, rows_dev, WIDTH), serial_blocks[:, :, None], axis=1)
    places = jnp.take_along_axis(coords.reshape(3, BLOCKS, rows_dev), serial_blocks[None], axis=2).astype(jnp.float32)
    placed = jnp.take_along_axis(cells.reshape(BLOCKS, rows_dev), serial_blocks, axis=1)
    ghost_lists = ghosts.reshape(BLOCKS, SLOTS)
    cell_total = XPLANES * YROWS * GRID

    def face(source, slot_no, axis_number, amount):
        row_block = lax.dynamic_index_in_dim(ordered, source, 0, keepdims=False)[slot_no * PATCH:(slot_no + 1) * PATCH]
        place_block = lax.dynamic_index_in_dim(places, source, 1, keepdims=False)[:, slot_no * PATCH:(slot_no + 1) * PATCH]
        return ghost_pair(row_block, shifted(place_block, axis_number, amount), ln1_gain, w_qkv, pos_proj, WIDTH)

    def one_block(block_no):
        slab_no = block_no // SUBS
        sub_no = block_no % SUBS
        first_x = (slab_no == 0).astype(jnp.float32)
        last_x = (slab_no == SLABS - 1).astype(jnp.float32)
        first_y = (sub_no == 0).astype(jnp.float32)
        last_y = (sub_no == SUBS - 1).astype(jnp.float32)
        pairs = [face((slab_no - 1) % SLABS * SUBS + sub_no, 1, 0, -first_x), face((slab_no + 1) % SLABS * SUBS + sub_no, 0, 0, last_x), face(slab_no * SUBS + (sub_no - 1) % SUBS, 1, 1, -first_y), face(slab_no * SUBS + (sub_no + 1) % SUBS, 0, 1, last_y)]
        blank = jnp.zeros((PATCH, WIDTH), jnp.bfloat16)
        table_keys = jnp.stack([blank] + [pair[0] for pair in pairs])
        table_values = jnp.stack([blank] + [pair[1] for pair in pairs])
        own_rows = lax.dynamic_index_in_dim(ordered, block_no, 0, keepdims=False)
        own_places = lax.dynamic_index_in_dim(places, block_no, 1, keepdims=False)
        normed = normalize(own_rows, ln1_gain).astype(jnp.bfloat16)
        qkv_base = jnp.dot(normed, w_qkv, preferred_element_type=jnp.float32)
        lifted = position_term(own_places, pos_proj)
        query_rows = (qkv_base[:, :WIDTH] + lifted[:, :WIDTH]).astype(jnp.bfloat16)
        key_rows = (qkv_base[:, WIDTH:2 * WIDTH] + lifted[:, WIDTH:]).astype(jnp.bfloat16)
        value_rows = qkv_base[:, 2 * WIDTH:].astype(jnp.bfloat16)
        limit = lax.dynamic_index_in_dim(counts, block_no, 0, keepdims=False)
        choices_here = lax.dynamic_index_in_dim(ghost_lists, block_no, 0, keepdims=False)

        def one_patch(slot_no):
            start = slot_no * PATCH

            def take(array):
                return lax.dynamic_slice_in_dim(array, start, PATCH, 0)
            picked = choices_here[slot_no]
            present = (picked > 0).astype(jnp.float32)
            ghost_keys = lax.dynamic_index_in_dim(table_keys, picked, 0, keepdims=False)
            ghost_values = lax.dynamic_index_in_dim(table_values, picked, 0, keepdims=False)
            attended = attend(take(query_rows), take(key_rows), take(value_rows), ghost_keys, ghost_values, present)
            result = finish(take(own_rows), attended, w_out, ln2_gain, w_up, w_down)
            return jnp.where(slot_no < limit, result, jnp.zeros_like(result))
        outputs = lax.map(one_patch, jnp.arange(SLOTS, dtype=jnp.int32)).reshape(rows_dev, WIDTH)
        cell_ids = lax.dynamic_index_in_dim(placed, block_no, 0, keepdims=False)
        cell_x = cell_ids // (GRID * GRID)
        cell_y = cell_ids // GRID % GRID
        cell_z = cell_ids % GRID
        local = ((cell_x - slab_no * XPLANES) * YROWS + (cell_y - sub_no * YROWS)) * GRID + cell_z
        live = jnp.arange(rows_dev, dtype=jnp.int32) // PATCH < limit
        target = jnp.where(live, local, cell_total).astype(jnp.int32)
        sums = jax.ops.segment_sum(outputs.astype(jnp.float32), target, cell_total + 1)[:cell_total]
        tally = jax.ops.segment_sum(live.astype(jnp.float32), target, cell_total + 1)[:cell_total]
        pooled = sums / jnp.maximum(tally, 1.0)[:, None]
        return (outputs, pooled)
    outputs, pooled = lax.map(one_block, jnp.arange(BLOCKS, dtype=jnp.int32))
    block_out = outputs.reshape(ROWS, WIDTH)
    pooled = pooled.reshape(SLABS, SUBS, XPLANES, YROWS, GRID, WIDTH).transpose(0, 2, 1, 3, 4, 5).reshape(GRID, GRID, GRID, WIDTH)
    return (block_out, pooled)
```

```python
import functools
import math

import jax
import jax.numpy as jnp
from jax import lax
from jax.experimental import pallas as pl
from jax.experimental.pallas import tpu as pltpu
from jax.sharding import PartitionSpec as P

HEADS = 4
GRID = 64
EPS = 1e-05
CHUNK = 256
SCALE = math.log2(math.e) / math.sqrt(32.0)
F32 = jnp.float32
BF16 = jnp.bfloat16
VMEM_LIMIT = 56 * 1024 * 1024


def dot(a, b, dims):
    return lax.dot_general(a, b, (dims, ((), ())), preferred_element_type=F32)


def normed_rows(values, gain):
    center = values - jnp.mean(values, axis=-1, keepdims=True)
    spread = jnp.mean(center * center, axis=-1, keepdims=True)
    return (center * lax.rsqrt(spread + EPS) * gain).astype(BF16)


def gather_kernel(first, rows, send, serial, feats, coords, cells, *refs):
    if send:
        ordered, aux, face0, face1, table, extra, picked, picked_extra, lines = refs
    else:
        ordered, aux, table, extra, picked, picked_extra, lines = refs
    table[...] = feats[...].astype(F32)
    cell = cells[...]
    lines[0:3, :] = coords[...].astype(F32)
    lines[3:4, :] = (((cell >> 12) & 3) * 8 + ((cell >> 6) & 7)).astype(F32)
    lines[4:5, :] = (cell & 63).astype(F32)
    lines[5:8, :] = jnp.zeros_like(lines[5:8, :])
    source = lax.broadcasted_iota(jnp.int32, (8, 128), 0)
    lane = lax.broadcasted_iota(jnp.int32, (8, 128), 1)
    place_spot = jnp.where((lane < 9) & (lane % 3 == source), 1.0, 0.0)
    cell_spot = jnp.where((lane == source + 6) & (source < 5), 1.0, 0.0)
    spot = jnp.where(source < 3, place_spot, cell_spot).astype(BF16)
    extra[...] = dot(lines[...].astype(BF16), spot, ((0,), (0,)))

    def step(block, carry):
        base = pl.multiple_of(block * 16, 16)
        for r in range(16):
            at = serial[first + base + r]
            picked[pl.ds(base + r, 1), :] = table[pl.ds(at, 1), :]
            picked_extra[pl.ds(base + r, 1), :] = extra[pl.ds(at, 1), :]
        return carry

    lax.fori_loop(0, rows // 16, step, 0)
    ordered[...] = picked[...].astype(BF16)
    aux[...] = picked_extra[...].astype(BF16)
    if send:
        row = lax.broadcasted_iota(jnp.int32, (16, 128), 0)
        lane = lax.broadcasted_iota(jnp.int32, (16, 128), 1)
        pick = jnp.where((row == lane) & (row < 9), 1.0, 0.0).astype(BF16)
        patch = rows // 2
        for face, start in ((face0, 0), (face1, patch)):
            face[0:patch, :] = ordered[start : start + patch, :]
            line = dot(pick, aux[start : start + patch, :], ((1,), (1,))).astype(BF16)
            for c in range(patch // 128):
                face[patch + c * 16 : patch + c * 16 + 16, :] = line[:, c * 128 : c * 128 + 128]


def gather_rows(serial, feats, coords, cells, first, rows, send):
    total, width = feats.shape
    shapes = [jax.ShapeDtypeStruct((rows, width), BF16), jax.ShapeDtypeStruct((rows, 128), BF16)]
    if send:
        patch = rows // 2
        shapes += [jax.ShapeDtypeStruct((patch + patch // 8, width), BF16)] * 2
    vm = pl.BlockSpec(memory_space=pltpu.VMEM)
    return pl.pallas_call(
        functools.partial(gather_kernel, first, rows, send),
        in_specs=[pl.BlockSpec(memory_space=pltpu.SMEM), vm, vm, vm],
        out_specs=[vm] * len(shapes),
        out_shape=shapes,
        scratch_shapes=[
            pltpu.VMEM((total, width), F32),
            pltpu.VMEM((total, 128), F32),
            pltpu.VMEM((rows, width), F32),
            pltpu.VMEM((rows, 128), F32),
            pltpu.VMEM((8, total), F32),
        ],
        compiler_params=pltpu.CompilerParams(vmem_limit_bytes=VMEM_LIMIT),
        name="gather_rows",
    )(serial, feats, coords, cells)


def block_kernel(
    counts, ghosts, near, far, near_aux, far_aux, face1, face2, face3, face4,
    gain1, w_qkv, pos_proj, w_out, gain2, w_up, w_down,
    out, pooled,
    w_full, keys, values, faces, rows_all, cell_lines, sems,
):
    slot = pl.program_id(0)
    patch, width = out.shape
    slots = ghosts.shape[0]
    depth = width // HEADS
    sources = (face1, face2, face3, face4)

    @pl.when(slot == 0)
    def start():
        for j in range(slots):
            for g in range(4):
                @pl.when((j < counts[0]) & (ghosts[j] == g + 1))
                def fetch():
                    pltpu.make_async_copy(sources[g], faces.at[j], sems.at[j]).start()
        w_full[0:width, :] = w_qkv[...]
        pos = pos_proj[...]
        high = pos.astype(BF16).astype(F32)
        rest = pos - high
        middle = rest.astype(BF16).astype(F32)
        low = rest - middle
        blank = jnp.zeros((16 - 9, 2 * width), F32)
        stacked = jnp.concatenate([high, middle, low, blank], axis=0).astype(BF16)
        w_full[width : width + 16, 0 : 2 * width] = stacked
        w_full[width : width + 16, 2 * width :] = jnp.zeros((16, width), BF16)
        w_full[width + 16 :, :] = jnp.zeros((112, 3 * width), BF16)
        values[:, width:] = jnp.ones((2 * patch, width), BF16)

    live = slot < counts[0]
    base = pl.multiple_of(slot * patch, patch)

    @pl.when(jnp.logical_not(live))
    def dead():
        out[...] = jnp.zeros_like(out)
        rows_all[pl.ds(base, patch), :] = jnp.zeros((patch, 2 * width), BF16)
        cell_lines[:, pl.ds(base, patch)] = jnp.full((8, patch), -1.0, F32)

    def attend(ordered, query, count):
        lane = lax.broadcasted_iota(jnp.int32, (CHUNK, width), 1)
        for c in range(patch // CHUNK):
            lower = c * CHUNK
            q = query[lower : lower + CHUNK]
            mixed = jnp.zeros((CHUNK, width), F32)
            for h in range(HEADS):
                mine = (lane >= h * depth) & (lane < (h + 1) * depth)
                qh = jnp.where(mine, q, jnp.zeros_like(q))
                scores = dot(qh, keys[0:count, :], ((1,), (1,)))
                top = jnp.max(scores, axis=-1, keepdims=True)
                weights = jnp.exp2((scores - top) * SCALE).astype(BF16)
                summed = dot(weights, values[0:count, :], ((1,), (0,)))
                mixed = jnp.where(mine, summed[:, :width] / summed[:, width:], mixed)
            stream = (
                ordered[lower : lower + CHUNK] + dot(mixed.astype(BF16), w_out[...], ((1,), (0,)))
            ).astype(BF16)
            wide = stream.astype(F32)
            normed2 = normed_rows(wide, gain2[...])
            inner = jax.nn.gelu(dot(normed2, w_up[...], ((1,), (0,)))).astype(BF16)
            result = (wide + dot(inner, w_down[...], ((1,), (0,)))).astype(BF16)
            out[lower : lower + CHUNK, :] = result
            rows_all[pl.ds(base + lower, CHUNK), 0:width] = result

    @pl.when(live)
    def work():
        is_near = slot < 2
        ordered = jnp.where(is_near, near[...], far[...]).astype(F32)
        aux = jnp.where(is_near, near_aux[...].astype(F32), far_aux[...].astype(F32)).astype(BF16)
        normed = normed_rows(ordered, gain1[...])
        qkv = dot(jnp.concatenate([normed, aux], axis=1), w_full[...], ((1,), (0,)))
        query = qkv[:, :width].astype(BF16)
        keys[0:patch, :] = qkv[:, width : 2 * width].astype(BF16)
        values[0:patch, 0:width] = qkv[:, 2 * width :].astype(BF16)
        rows_all[pl.ds(base, patch), width:] = jnp.ones((patch, width), BF16)
        row = lax.broadcasted_iota(jnp.int32, (8, 128), 0)
        lane = lax.broadcasted_iota(jnp.int32, (8, 128), 1)
        pick = jnp.where(lane == 9, 64.0, jnp.where(lane == 10, 1.0, 0.0)).astype(BF16)
        cell_lines[:, pl.ds(base, patch)] = dot(pick, aux, ((1,), (1,)))
        ghost = ghosts[slot]

        @pl.when(ghost > 0)
        def with_ghost():
            pltpu.make_async_copy(face1, faces.at[slot], sems.at[slot]).wait()
            there = normed_rows(faces[slot, 0:patch, :].astype(F32), gain1[...])
            line = jnp.concatenate(
                [faces[slot, patch + c * 16 : patch + c * 16 + 16, :] for c in range(patch // 128)],
                axis=1,
            )
            slab_no = lax.axis_index("slab")
            sub_no = lax.axis_index("sub")
            on_x = ghost < 3
            down = (ghost == 1) | (ghost == 3)
            place = jnp.where(on_x, slab_no, sub_no)
            edge = jnp.where(down, 0, jnp.where(on_x, lax.axis_size("slab"), lax.axis_size("sub")) - 1)
            amount = jnp.where(place == edge, jnp.where(down, -1.0, 1.0), 0.0)
            bump = jnp.where(on_x, pos_proj[0:1, width:], pos_proj[1:2, width:]) * amount
            both = dot(there, w_full[0:width, width:], ((1,), (0,)))
            lifted = dot(line, w_full[width : width + 16, width : 2 * width], ((0,), (0,)))
            keys[patch:, :] = (both[:, :width] + (lifted + bump)).astype(BF16)
            values[patch:, 0:width] = both[:, width:].astype(BF16)
            attend(ordered, query, 2 * patch)

        @pl.when(ghost == 0)
        def without_ghost():
            attend(ordered, query, patch)

    @pl.when(slot == slots - 1)
    def pool():
        cells_total = pooled.shape[0]
        for c in range(cells_total // 256):
            ids = (lax.broadcasted_iota(jnp.int32, (256, 1), 0) + c * 256).astype(F32)
            onehot = jnp.where(cell_lines[0:1, :] == ids, 1.0, 0.0).astype(BF16)
            summed = dot(onehot, rows_all[...], ((1,), (0,)))
            pooled[c * 256 : c * 256 + 256, :] = summed[:, :width] / jnp.maximum(summed[:, width:], 1.0)


def run_block(counts, ghosts, near, far, near_aux, far_aux, faces, gain1, w_qkv, pos_proj, w_out, gain2, w_up, w_down, cells_total):
    slots = ghosts.shape[0]
    width = near.shape[1]
    patch = near.shape[0] // 2
    smem = pl.BlockSpec(memory_space=pltpu.SMEM)
    vm = pl.BlockSpec(memory_space=pltpu.VMEM)
    hbm = pl.BlockSpec(memory_space=pl.ANY)
    near_spec = pl.BlockSpec((patch, width), lambda j: (jnp.minimum(j, 1), 0))
    far_spec = pl.BlockSpec((patch, width), lambda j: (jnp.maximum(j - 2, 0), 0))
    return pl.pallas_call(
        block_kernel,
        grid=(slots,),
        in_specs=[smem, smem, near_spec, far_spec, near_spec, far_spec, hbm, hbm, hbm, hbm] + [vm] * 7,
        out_specs=[
            pl.BlockSpec((patch, width), lambda j: (j, 0)),
            pl.BlockSpec((cells_total, width), lambda j: (0, 0)),
        ],
        out_shape=[
            jax.ShapeDtypeStruct((slots * patch, width), BF16),
            jax.ShapeDtypeStruct((cells_total, width), F32),
        ],
        scratch_shapes=[
            pltpu.VMEM((2 * width, 3 * width), BF16),
            pltpu.VMEM((2 * patch, width), BF16),
            pltpu.VMEM((2 * patch, 2 * width), BF16),
            pltpu.VMEM((slots,) + faces[0].shape, BF16),
            pltpu.VMEM((slots * patch, 2 * width), BF16),
            pltpu.VMEM((8, slots * patch), F32),
            pltpu.SemaphoreType.DMA((slots,)),
        ],
        compiler_params=pltpu.CompilerParams(vmem_limit_bytes=VMEM_LIMIT),
        name="patch_block",
    )(counts, ghosts, near, far, near_aux, far_aux, *faces, gain1, w_qkv, pos_proj, w_out, gain2, w_up, w_down)


def per_device(
    feats, coords, serial, cells, counts, ghosts, ln1_gain, w_qkv, pos_proj, w_out, ln2_gain, w_up, w_down
):
    rows_dev, width = feats.shape
    patch = rows_dev // ghosts.shape[0]
    slab_total = lax.axis_size("slab")
    sub_total = lax.axis_size("sub")
    cells2 = cells.reshape(1, rows_dev)
    near, near_aux, face0, face1 = gather_rows(serial, feats, coords, cells2, 0, 2 * patch, True)
    far, far_aux = gather_rows(serial, feats, coords, cells2, 2 * patch, rows_dev - 2 * patch, False)

    def ring(axis, size):
        up = [(i, (i + 1) % size) for i in range(size)]
        down = [(j, i) for i, j in up]
        return [lax.ppermute(face1, axis, up), lax.ppermute(face0, axis, down)]

    faces = ring("slab", slab_total) + ring("sub", sub_total)
    planes = GRID // slab_total
    lines = GRID // sub_total
    out, pooled = run_block(
        counts, ghosts, near, far, near_aux, far_aux, faces,
        ln1_gain.reshape(1, width), w_qkv, pos_proj, w_out, ln2_gain.reshape(1, width), w_up, w_down,
        planes * lines * GRID,
    )
    return out, pooled.reshape(planes, lines, GRID, width)


def solution(mesh):
    rows = P(("slab", "sub"))
    specs = (P(("slab", "sub"), None), P(None, ("slab", "sub")), rows, rows, rows, rows) + (P(),) * 7
    return jax.shard_map(
        per_device,
        mesh=mesh,
        in_specs=specs,
        out_specs=(P(("slab", "sub"), None), P("slab", "sub", None, None)),
        check_vma=False,
    )
```

```python
import functools
import math

import jax
import jax.numpy as jnp
from jax import lax
from jax.experimental import pallas as pl
from jax.experimental.pallas import tpu as pltpu
from jax.sharding import PartitionSpec as P

HEADS = 4
GRID = 64
EPS = 1e-05
CHUNK = 256
SCALE = math.log2(math.e) / math.sqrt(32.0)
F32 = jnp.float32
BF16 = jnp.bfloat16
VMEM_LIMIT = 56 * 1024 * 1024


def dot(a, b, dims):
    return lax.dot_general(a, b, (dims, ((), ())), preferred_element_type=F32)


def normed_rows(values, gain):
    center = values - jnp.mean(values, axis=-1, keepdims=True)
    spread = jnp.mean(center * center, axis=-1, keepdims=True)
    return (center * lax.rsqrt(spread + EPS) * gain).astype(BF16)


def full_weights(w_full, w_qkv, pos_proj):
    width = w_qkv.shape[0]
    pos = pos_proj[...]
    high = pos.astype(BF16).astype(F32)
    rest = pos - high
    middle = rest.astype(BF16).astype(F32)
    low = rest - middle
    blank = jnp.zeros((16 - 9, 2 * width), F32)
    stacked = jnp.concatenate([high, middle, low, blank], axis=0).astype(BF16)
    w_full[0:width, :] = w_qkv[...]
    w_full[width : width + 16, 0 : 2 * width] = stacked
    w_full[width : width + 16, 2 * width :] = jnp.zeros((16, width), BF16)
    if w_full.shape[0] > width + 16:
        w_full[width + 16 :, :] = jnp.zeros((width - 16, 3 * width), BF16)


def pick_rows(first, rows, serial, feats, coords, cells, table, extra, picked, picked_extra, lines):
    table[...] = feats[...].astype(F32)
    cell = cells[...]
    lines[0:3, :] = coords[...].astype(F32)
    lines[3:4, :] = (((cell >> 12) & 3) * 8 + ((cell >> 6) & 7)).astype(F32)
    lines[4:5, :] = (cell & 63).astype(F32)
    lines[5:8, :] = jnp.zeros_like(lines[5:8, :])
    source = lax.broadcasted_iota(jnp.int32, (8, 128), 0)
    lane = lax.broadcasted_iota(jnp.int32, (8, 128), 1)
    place_spot = jnp.where((lane < 9) & (lane % 3 == source), 1.0, 0.0)
    cell_spot = jnp.where((lane == source + 6) & (source < 5), 1.0, 0.0)
    spot = jnp.where(source < 3, place_spot, cell_spot).astype(BF16)
    extra[...] = dot(lines[...].astype(BF16), spot, ((0,), (0,)))

    def step(block, carry):
        base = pl.multiple_of(block * 16, 16)
        for r in range(16):
            at = serial[first + base + r]
            picked[pl.ds(base + r, 1), :] = table[pl.ds(at, 1), :]
            picked_extra[pl.ds(base + r, 1), :] = extra[pl.ds(at, 1), :]
        return carry

    lax.fori_loop(0, rows // 16, step, 0)


def near_kernel(rows, serial, feats, coords, cells, ordered, aux, face0, face1, table, extra, picked, picked_extra, lines):
    pick_rows(0, rows, serial, feats, coords, cells, table, extra, picked, picked_extra, lines)
    ordered[...] = picked[...].astype(BF16)
    aux[...] = picked_extra[...].astype(BF16)
    row = lax.broadcasted_iota(jnp.int32, (16, 128), 0)
    lane = lax.broadcasted_iota(jnp.int32, (16, 128), 1)
    pick = jnp.where((row == lane) & (row < 9), 1.0, 0.0).astype(BF16)
    patch = rows // 2
    for face, start in ((face0, 0), (face1, patch)):
        face[0:patch, :] = ordered[start : start + patch, :]
        line = dot(pick, aux[start : start + patch, :], ((1,), (1,))).astype(BF16)
        for c in range(patch // 128):
            face[patch + c * 16 : patch + c * 16 + 16, :] = line[:, c * 128 : c * 128 + 128]


def far_kernel(
    first, serial, feats, coords, cells, near, near_aux, gain1, w_qkv, pos_proj,
    ordered, query, keys, values, cell_lines,
    table, extra, picked, picked_extra, lines, w_full,
):
    total, width = feats.shape
    full_weights(w_full, w_qkv, pos_proj)
    pick_rows(first, total - first, serial, feats, coords, cells, table, extra, picked, picked_extra, lines)
    row = lax.broadcasted_iota(jnp.int32, (8, 128), 0)
    lane = lax.broadcasted_iota(jnp.int32, (8, 128), 1)
    pick = jnp.where(lane == 9, 64.0, jnp.where(lane == 10, 1.0, 0.0)).astype(BF16)
    block = 512
    for lower in range(0, total, block):
        span = slice(lower, lower + block)
        if lower < first:
            wide = near[span, :].astype(F32)
            aux = near_aux[span, :]
            ordered[span, :] = near[span, :]
        else:
            wide = picked[lower - first : lower - first + block, :]
            aux = picked_extra[lower - first : lower - first + block, :].astype(BF16)
            ordered[span, :] = wide.astype(BF16)
        normed = normed_rows(wide, gain1[...])
        qkv = dot(jnp.concatenate([normed, aux], axis=1), w_full[...], ((1,), (0,)))
        query[span, :] = qkv[:, :width].astype(BF16)
        keys[span, :] = qkv[:, width : 2 * width].astype(BF16)
        values[span, :] = qkv[:, 2 * width :].astype(BF16)
        cell_lines[:, span] = dot(pick, aux, ((1,), (1,)))


def gather_scratch(total, width, rows):
    return [
        pltpu.VMEM((total, width), F32),
        pltpu.VMEM((total, 128), F32),
        pltpu.VMEM((rows, width), F32),
        pltpu.VMEM((rows, 128), F32),
        pltpu.VMEM((8, total), F32),
    ]


def gather_near(serial, feats, coords, cells, rows):
    total, width = feats.shape
    patch = rows // 2
    vm = pl.BlockSpec(memory_space=pltpu.VMEM)
    return pl.pallas_call(
        functools.partial(near_kernel, rows),
        in_specs=[pl.BlockSpec(memory_space=pltpu.SMEM), vm, vm, vm],
        out_specs=[vm] * 4,
        out_shape=[jax.ShapeDtypeStruct((rows, width), BF16), jax.ShapeDtypeStruct((rows, 128), BF16)]
        + [jax.ShapeDtypeStruct((patch + patch // 8, width), BF16)] * 2,
        scratch_shapes=gather_scratch(total, width, rows),
        compiler_params=pltpu.CompilerParams(vmem_limit_bytes=VMEM_LIMIT),
        name="gather_near",
    )(serial, feats, coords, cells)


def gather_far(serial, feats, coords, cells, near, near_aux, gain1, w_qkv, pos_proj):
    total, width = feats.shape
    first = near.shape[0]
    vm = pl.BlockSpec(memory_space=pltpu.VMEM)
    return pl.pallas_call(
        functools.partial(far_kernel, first),
        in_specs=[pl.BlockSpec(memory_space=pltpu.SMEM)] + [vm] * 8,
        out_specs=[vm] * 5,
        out_shape=[jax.ShapeDtypeStruct((total, width), BF16)] * 4 + [jax.ShapeDtypeStruct((8, total), F32)],
        scratch_shapes=gather_scratch(total, width, total - first) + [pltpu.VMEM((2 * width, 3 * width), BF16)],
        compiler_params=pltpu.CompilerParams(vmem_limit_bytes=VMEM_LIMIT),
        name="gather_far",
    )(serial, feats, coords, cells, near, near_aux, gain1, w_qkv, pos_proj)


def block_kernel(
    counts, ghosts, ordered, query, own_keys, own_values, cell_lines, face1, face2, face3, face4,
    gain1, w_qkv, pos_proj, w_out, gain2, w_up, w_down,
    out, pooled,
    w_full, keys, values, faces, rows_all, sems,
):
    slot = pl.program_id(0)
    patch, width = out.shape
    slots = ghosts.shape[0]
    depth = width // HEADS
    sources = (face1, face2, face3, face4)

    @pl.when(slot == 0)
    def start():
        for j in range(slots):
            for g in range(4):
                @pl.when((j < counts[0]) & (ghosts[j] == g + 1))
                def fetch():
                    pltpu.make_async_copy(sources[g], faces.at[j], sems.at[j]).start()
        full_weights(w_full, w_qkv, pos_proj)
        values[:, width:] = jnp.ones((2 * patch, width), BF16)

    live = slot < counts[0]
    base = pl.multiple_of(slot * patch, patch)

    @pl.when(jnp.logical_not(live))
    def dead():
        out[...] = jnp.zeros_like(out)
        rows_all[pl.ds(base, patch), :] = jnp.zeros((patch, 2 * width), BF16)

    def finish(lower, mixed):
        stream = (
            ordered[lower : lower + CHUNK, :].astype(F32) + dot(mixed.astype(BF16), w_out[...], ((1,), (0,)))
        ).astype(BF16)
        yield
        wide = stream.astype(F32)
        normed2 = normed_rows(wide, gain2[...])
        yield
        inner = jax.nn.gelu(dot(normed2, w_up[...], ((1,), (0,)))).astype(BF16)
        yield
        result = (wide + dot(inner, w_down[...], ((1,), (0,)))).astype(BF16)
        out[lower : lower + CHUNK, :] = result
        rows_all[pl.ds(base + lower, CHUNK), 0:width] = result
        yield

    def attend(count):
        lane = lax.broadcasted_iota(jnp.int32, (CHUNK, width), 1)
        tail = iter(())
        for c in range(patch // CHUNK):
            lower = c * CHUNK
            q = query[lower : lower + CHUNK, :]
            mixed = jnp.zeros((CHUNK, width), F32)
            for h in range(HEADS):
                mine = (lane >= h * depth) & (lane < (h + 1) * depth)
                qh = jnp.where(mine, q, jnp.zeros_like(q))
                scores = dot(qh, keys[0:count, :], ((1,), (1,)))
                next(tail, None)
                top = jnp.max(scores, axis=-1, keepdims=True)
                weights = jnp.exp2((scores - top) * SCALE).astype(BF16)
                summed = dot(weights, values[0:count, :], ((1,), (0,)))
                mixed = jnp.where(mine, summed[:, :width] / summed[:, width:], mixed)
            tail = finish(lower, mixed)
        for _ in tail:
            pass

    @pl.when(live)
    def work():
        keys[0:patch, :] = own_keys[...]
        values[0:patch, 0:width] = own_values[...]
        rows_all[pl.ds(base, patch), width:] = jnp.ones((patch, width), BF16)
        ghost = ghosts[slot]

        @pl.when(ghost > 0)
        def with_ghost():
            pltpu.make_async_copy(face1, faces.at[slot], sems.at[slot]).wait()
            there = normed_rows(faces[slot, 0:patch, :].astype(F32), gain1[...])
            line = jnp.concatenate(
                [faces[slot, patch + c * 16 : patch + c * 16 + 16, :] for c in range(patch // 128)],
                axis=1,
            )
            slab_no = lax.axis_index("slab")
            sub_no = lax.axis_index("sub")
            on_x = ghost < 3
            down = (ghost == 1) | (ghost == 3)
            place = jnp.where(on_x, slab_no, sub_no)
            edge = jnp.where(down, 0, jnp.where(on_x, lax.axis_size("slab"), lax.axis_size("sub")) - 1)
            amount = jnp.where(place == edge, jnp.where(down, -1.0, 1.0), 0.0)
            bump = jnp.where(on_x, pos_proj[0:1, width:], pos_proj[1:2, width:]) * amount
            both = dot(there, w_full[0:width, width:], ((1,), (0,)))
            lifted = dot(line, w_full[width : width + 16, width : 2 * width], ((0,), (0,)))
            keys[patch:, :] = (both[:, :width] + (lifted + bump)).astype(BF16)
            values[patch:, 0:width] = both[:, width:].astype(BF16)
            attend(2 * patch)

        @pl.when(ghost == 0)
        def without_ghost():
            attend(patch)

    @pl.when(slot == slots - 1)
    def pool():
        cells_total = pooled.shape[0]
        row_no = lax.broadcasted_iota(jnp.int32, (1, slots * patch), 1)
        line = jnp.where(row_no < counts[0] * patch, cell_lines[0:1, :], -1.0)
        for c in range(cells_total // 256):
            ids = (lax.broadcasted_iota(jnp.int32, (256, 1), 0) + c * 256).astype(F32)
            onehot = jnp.where(line == ids, 1.0, 0.0).astype(BF16)
            summed = dot(onehot, rows_all[...], ((1,), (0,)))
            pooled[c * 256 : c * 256 + 256, :] = summed[:, :width] / jnp.maximum(summed[:, width:], 1.0)


def run_block(counts, ghosts, ordered, query, own_keys, own_values, cell_lines, faces, gain1, w_qkv, pos_proj, w_out, gain2, w_up, w_down, cells_total):
    slots = ghosts.shape[0]
    width = ordered.shape[1]
    patch = ordered.shape[0] // slots
    smem = pl.BlockSpec(memory_space=pltpu.SMEM)
    vm = pl.BlockSpec(memory_space=pltpu.VMEM)
    hbm = pl.BlockSpec(memory_space=pl.ANY)
    part = pl.BlockSpec((patch, width), lambda j: (j, 0))
    return pl.pallas_call(
        block_kernel,
        grid=(slots,),
        in_specs=[smem, smem] + [part] * 4 + [vm] + [hbm] * 4 + [vm] * 7,
        out_specs=[part, pl.BlockSpec((cells_total, width), lambda j: (0, 0))],
        out_shape=[
            jax.ShapeDtypeStruct((slots * patch, width), BF16),
            jax.ShapeDtypeStruct((cells_total, width), F32),
        ],
        scratch_shapes=[
            pltpu.VMEM((width + 16, 3 * width), BF16),
            pltpu.VMEM((2 * patch, width), BF16),
            pltpu.VMEM((2 * patch, 2 * width), BF16),
            pltpu.VMEM((slots,) + faces[0].shape, BF16),
            pltpu.VMEM((slots * patch, 2 * width), BF16),
            pltpu.SemaphoreType.DMA((slots,)),
        ],
        compiler_params=pltpu.CompilerParams(vmem_limit_bytes=VMEM_LIMIT),
        name="patch_block",
    )(counts, ghosts, ordered, query, own_keys, own_values, cell_lines, *faces, gain1, w_qkv, pos_proj, w_out, gain2, w_up, w_down)


def per_device(
    feats, coords, serial, cells, counts, ghosts, ln1_gain, w_qkv, pos_proj, w_out, ln2_gain, w_up, w_down
):
    rows_dev, width = feats.shape
    patch = rows_dev // ghosts.shape[0]
    slab_total = lax.axis_size("slab")
    sub_total = lax.axis_size("sub")
    cells2 = cells.reshape(1, rows_dev)
    gain1 = ln1_gain.reshape(1, width)
    near, near_aux, face0, face1 = gather_near(serial, feats, coords, cells2, 2 * patch)
    own = gather_far(serial, feats, coords, cells2, near, near_aux, gain1, w_qkv, pos_proj)

    def ring(axis, size):
        up = [(i, (i + 1) % size) for i in range(size)]
        down = [(j, i) for i, j in up]
        return [lax.ppermute(face1, axis, up), lax.ppermute(face0, axis, down)]

    faces = ring("slab", slab_total) + ring("sub", sub_total)
    planes = GRID // slab_total
    lines = GRID // sub_total
    out, pooled = run_block(
        counts, ghosts, *own, faces,
        gain1, w_qkv, pos_proj, w_out, ln2_gain.reshape(1, width), w_up, w_down,
        planes * lines * GRID,
    )
    return out, pooled.reshape(planes, lines, GRID, width)


def solution(mesh):
    rows = P(("slab", "sub"))
    specs = (P(("slab", "sub"), None), P(None, ("slab", "sub")), rows, rows, rows, rows) + (P(),) * 7
    return jax.shard_map(
        per_device,
        mesh=mesh,
        in_specs=specs,
        out_specs=(P(("slab", "sub"), None), P("slab", "sub", None, None)),
        check_vma=False,
    )
```

```python
import functools
import math

import jax
import jax.numpy as jnp
from jax import lax
from jax.experimental import pallas as pl
from jax.experimental.pallas import tpu as pltpu
from jax.sharding import PartitionSpec as P

HEADS = 4
GRID = 64
EPS = 1e-05
CHUNK = 256
SCALE = math.log2(math.e) / math.sqrt(32.0)
F32 = jnp.float32
BF16 = jnp.bfloat16
VMEM_LIMIT = 24 * 1024 * 1024


def dot(a, b, dims):
    return lax.dot_general(a, b, (dims, ((), ())), preferred_element_type=F32)


def normed_rows(values, gain):
    center = values - jnp.mean(values, axis=-1, keepdims=True)
    spread = jnp.mean(center * center, axis=-1, keepdims=True)
    return (center * lax.rsqrt(spread + EPS) * gain).astype(BF16)


def full_weights(w_full, w_qkv, pos_proj):
    width = w_qkv.shape[0]
    pos = pos_proj[...]
    high = pos.astype(BF16).astype(F32)
    rest = pos - high
    middle = rest.astype(BF16).astype(F32)
    low = rest - middle
    blank = jnp.zeros((16 - 9, 2 * width), F32)
    stacked = jnp.concatenate([high, middle, low, blank], axis=0).astype(BF16)
    w_full[0:width, 0 : 3 * width] = w_qkv[...]
    w_full[width : width + 16, 0 : 2 * width] = stacked
    w_full[width : width + 16, 2 * width : 3 * width] = jnp.zeros((16, width), BF16)
    if w_full.shape[0] > width + 16:
        w_full[width + 16 :, 0 : 3 * width] = jnp.zeros((width - 16, 3 * width), BF16)


def build_tables(feats, coords, cells, table, extra, lines):
    table[...] = feats[...].astype(F32)
    cell = cells[...]
    lines[0:3, :] = coords[...].astype(F32)
    lines[3:4, :] = (((cell >> 12) & 3) * 8 + ((cell >> 6) & 7)).astype(F32)
    lines[4:5, :] = (cell & 63).astype(F32)
    lines[5:6, :] = ((cell >> 13) & 1).astype(F32)
    lines[6:8, :] = jnp.zeros_like(lines[6:8, :])
    source = lax.broadcasted_iota(jnp.int32, (8, 128), 0)
    lane = lax.broadcasted_iota(jnp.int32, (8, 128), 1)
    place_spot = jnp.where((lane < 9) & (lane % 3 == source), 1.0, 0.0)
    cell_spot = jnp.where((lane == source + 6) & (source < 6), 1.0, 0.0)
    spot = jnp.where(source < 3, place_spot, cell_spot).astype(BF16)
    extra[...] = dot(lines[...].astype(BF16), spot, ((0,), (0,)))


def pick_rows(first, rows, serial, table, extra, picked, picked_extra):
    def step(block, carry):
        base = pl.multiple_of(block * 16, 16)
        for r in range(16):
            at = serial[first + base + r]
            picked[pl.ds(base + r, 1), :] = table[pl.ds(at, 1), :]
            picked_extra[pl.ds(base + r, 1), :] = extra[pl.ds(at, 1), :]
        return carry

    lax.fori_loop(0, rows // 16, step, 0)


def near_kernel(rows, serial, feats, coords, cells, ordered, aux, face0, face1, table, extra, picked, picked_extra, lines):
    build_tables(feats, coords, cells, table, extra, lines)
    pick_rows(0, rows, serial, table, extra, picked, picked_extra)
    ordered[...] = picked[...].astype(BF16)
    aux[...] = picked_extra[...].astype(BF16)
    row = lax.broadcasted_iota(jnp.int32, (16, 128), 0)
    lane = lax.broadcasted_iota(jnp.int32, (16, 128), 1)
    pick = jnp.where((row == lane) & (row < 9), 1.0, 0.0).astype(BF16)
    patch = rows // 2
    for face, start in ((face0, 0), (face1, patch)):
        face[0:patch, :] = ordered[start : start + patch, :]
        line = dot(pick, aux[start : start + patch, :], ((1,), (1,))).astype(BF16)
        for c in range(patch // 128):
            face[patch + c * 16 : patch + c * 16 + 16, :] = line[:, c * 128 : c * 128 + 128]


def far_kernel(
    first, serial, table, extra, near, near_aux, gain1, w_qkv, pos_proj,
    ordered, query, keys, values, side, cell_lines,
    picked, picked_extra, w_full,
):
    total, width = table.shape
    full_weights(w_full, w_qkv, pos_proj)
    row = lax.broadcasted_iota(jnp.int32, (width, width), 0)
    w_full[0:width, 3 * width :] = jnp.zeros((width, width), BF16)
    w_full[width:, 3 * width :] = jnp.where(row == 11, 1.0, 0.0).astype(BF16)
    pick_rows(first, total - first, serial, table, extra, picked, picked_extra)
    row = lax.broadcasted_iota(jnp.int32, (8, 128), 0)
    lane = lax.broadcasted_iota(jnp.int32, (8, 128), 1)
    pick = jnp.where((row < 3) & (lane == row + 9), 1.0, 0.0).astype(BF16)
    block = 512
    for lower in range(0, total, block):
        span = slice(lower, lower + block)
        if lower < first:
            wide = near[span, :].astype(F32)
            aux = near_aux[span, :]
            ordered[span, :] = near[span, :]
        else:
            wide = picked[lower - first : lower - first + block, :]
            aux = picked_extra[lower - first : lower - first + block, :].astype(BF16)
            ordered[span, :] = wide.astype(BF16)
        normed = normed_rows(wide, gain1[...])
        qkv = dot(jnp.concatenate([normed, aux], axis=1), w_full[...], ((1,), (0,)))
        query[span, :] = qkv[:, :width].astype(BF16)
        keys[span, :] = qkv[:, width : 2 * width].astype(BF16)
        values[span, :] = qkv[:, 2 * width : 3 * width].astype(BF16)
        side[span, :] = qkv[:, 3 * width :].astype(BF16)
        cell_lines[:, span] = dot(pick, aux, ((1,), (1,)))


def gather_near(serial, feats, coords, cells, rows):
    total, width = feats.shape
    patch = rows // 2
    vm = pl.BlockSpec(memory_space=pltpu.VMEM)
    return pl.pallas_call(
        functools.partial(near_kernel, rows),
        in_specs=[pl.BlockSpec(memory_space=pltpu.SMEM), vm, vm, vm],
        out_specs=[vm] * 6,
        out_shape=[jax.ShapeDtypeStruct((rows, width), BF16), jax.ShapeDtypeStruct((rows, 128), BF16)]
        + [jax.ShapeDtypeStruct((patch + patch // 8, width), BF16)] * 2
        + [jax.ShapeDtypeStruct((total, width), F32), jax.ShapeDtypeStruct((total, 128), F32)],
        scratch_shapes=[
            pltpu.VMEM((rows, width), F32),
            pltpu.VMEM((rows, 128), F32),
            pltpu.VMEM((8, total), F32),
        ],
        compiler_params=pltpu.CompilerParams(vmem_limit_bytes=VMEM_LIMIT),
        name="gather_near",
    )(serial, feats, coords, cells)


def gather_far(serial, table, extra, near, near_aux, gain1, w_qkv, pos_proj):
    total, width = table.shape
    first = near.shape[0]
    vm = pl.BlockSpec(memory_space=pltpu.VMEM)
    return pl.pallas_call(
        functools.partial(far_kernel, first),
        in_specs=[pl.BlockSpec(memory_space=pltpu.SMEM)] + [vm] * 7,
        out_specs=[vm] * 6,
        out_shape=[jax.ShapeDtypeStruct((total, width), BF16)] * 5 + [jax.ShapeDtypeStruct((8, total), F32)],
        scratch_shapes=[
            pltpu.VMEM((total - first, width), F32),
            pltpu.VMEM((total - first, 128), F32),
            pltpu.VMEM((2 * width, 4 * width), BF16),
        ],
        compiler_params=pltpu.CompilerParams(vmem_limit_bytes=VMEM_LIMIT),
        name="gather_far",
    )(serial, table, extra, near, near_aux, gain1, w_qkv, pos_proj)


def block_kernel(
    counts, ghosts, ordered, query, own_keys, own_values, side, cell_lines, face1, face2, face3, face4,
    gain1, w_qkv, pos_proj, w_out, gain2, w_up, w_down,
    out, pooled,
    w_full, keys, values, faces, rows_all, sems,
):
    slot = pl.program_id(0)
    patch, width = out.shape
    slots = ghosts.shape[0]
    depth = width // HEADS
    sources = (face1, face2, face3, face4)

    @pl.when(slot == 0)
    def start():
        for j in range(slots):
            for g in range(4):
                @pl.when((j < counts[0]) & (ghosts[j] == g + 1))
                def fetch():
                    pltpu.make_async_copy(sources[g], faces.at[j], sems.at[j]).start()
        full_weights(w_full, w_qkv, pos_proj)
        values[:, width:] = jnp.ones((2 * patch, width), BF16)

    live = slot < counts[0]
    base = pl.multiple_of(slot * patch, patch)

    @pl.when(jnp.logical_not(live))
    def dead():
        out[...] = jnp.zeros_like(out)
        rows_all[pl.ds(base, patch), :] = jnp.zeros((patch, 2 * width), BF16)

    def finish(lower, mixed):
        stream = (
            ordered[lower : lower + CHUNK, :].astype(F32) + dot(mixed.astype(BF16), w_out[...], ((1,), (0,)))
        ).astype(BF16)
        yield
        wide = stream.astype(F32)
        normed2 = normed_rows(wide, gain2[...])
        yield
        inner = jax.nn.gelu(dot(normed2, w_up[...], ((1,), (0,)))).astype(BF16)
        yield
        result = (wide + dot(inner, w_down[...], ((1,), (0,)))).astype(BF16)
        out[lower : lower + CHUNK, :] = result
        upper = side[lower : lower + CHUNK, :] > 0.5
        none = jnp.zeros_like(result)
        rows_all[pl.ds(base + lower, CHUNK), 0:width] = jnp.where(upper, none, result)
        rows_all[pl.ds(base + lower, CHUNK), width:] = jnp.where(upper, result, none)
        yield

    def attend(count):
        lane = lax.broadcasted_iota(jnp.int32, (CHUNK, width), 1)

        def head_scores(unit):
            lower = unit // HEADS * CHUNK
            h = unit % HEADS
            mine = (lane >= h * depth) & (lane < (h + 1) * depth)
            q = query[lower : lower + CHUNK, :]
            return mine, dot(jnp.where(mine, q, jnp.zeros_like(q)), keys[0:count, :], ((1,), (1,)))

        units = patch // CHUNK * HEADS
        tail = iter(())
        ahead = head_scores(0)
        mixed = jnp.zeros((CHUNK, width), F32)
        for unit in range(units):
            mine, scores = ahead
            if unit + 1 < units:
                ahead = head_scores(unit + 1)
            next(tail, None)
            top = jnp.max(scores, axis=-1, keepdims=True)
            weights = jnp.exp2((scores - top) * SCALE).astype(BF16)
            summed = dot(weights, values[0:count, :], ((1,), (0,)))
            mixed = jnp.where(mine, summed[:, :width] / summed[:, width:], mixed)
            if unit % HEADS == HEADS - 1:
                tail = finish(unit // HEADS * CHUNK, mixed)
        for _ in tail:
            pass

    @pl.when(live)
    def work():
        keys[0:patch, :] = own_keys[...]
        values[0:patch, 0:width] = own_values[...]
        ghost = ghosts[slot]

        @pl.when(ghost > 0)
        def with_ghost():
            pltpu.make_async_copy(face1, faces.at[slot], sems.at[slot]).wait()
            there = normed_rows(faces[slot, 0:patch, :].astype(F32), gain1[...])
            line = jnp.concatenate(
                [faces[slot, patch + c * 16 : patch + c * 16 + 16, :] for c in range(patch // 128)],
                axis=1,
            )
            slab_no = lax.axis_index("slab")
            sub_no = lax.axis_index("sub")
            on_x = ghost < 3
            down = (ghost == 1) | (ghost == 3)
            place = jnp.where(on_x, slab_no, sub_no)
            edge = jnp.where(down, 0, jnp.where(on_x, lax.axis_size("slab"), lax.axis_size("sub")) - 1)
            amount = jnp.where(place == edge, jnp.where(down, -1.0, 1.0), 0.0)
            bump = jnp.where(on_x, pos_proj[0:1, width:], pos_proj[1:2, width:]) * amount
            both = dot(there, w_full[0:width, width:], ((1,), (0,)))
            lifted = dot(line, w_full[width : width + 16, width : 2 * width], ((0,), (0,)))
            keys[patch:, :] = (both[:, :width] + (lifted + bump)).astype(BF16)
            values[patch:, 0:width] = both[:, width:].astype(BF16)
            attend(2 * patch)

        @pl.when(ghost == 0)
        def without_ghost():
            attend(patch)

    @pl.when(slot == slots - 1)
    def pool():
        half = pooled.shape[0] // 2
        row_no = lax.broadcasted_iota(jnp.int32, (1, slots * patch), 1)
        column = jnp.where(row_no < counts[0] * patch, cell_lines[0:1, :], -1.0)
        depth_no = cell_lines[1:2, :]
        ids = lax.broadcasted_iota(jnp.int32, (GRID, 1), 0).astype(F32)
        by_column = jnp.where(column == ids[0 : 2 * half // GRID], 1.0, 0.0).astype(BF16)
        by_depth = jnp.where(depth_no == ids, 1.0, 0.0).astype(BF16)
        tally = jnp.maximum(dot(by_depth, by_column, ((1,), (1,))), 1.0)
        lower_cell = (column - cell_lines[2:3, :] * (half // GRID)) * GRID + depth_no
        wide_ids = lax.broadcasted_iota(jnp.int32, (256, 1), 0).astype(F32)
        for c in range(half // 256):
            onehot = jnp.where(lower_cell == wide_ids + c * 256.0, 1.0, 0.0).astype(BF16)
            summed = dot(onehot, rows_all[...], ((1,), (0,)))
            for k in range(256 // GRID):
                part = summed[k * GRID : (k + 1) * GRID]
                for upper in range(2):
                    at = upper * (half // GRID) + c * (256 // GRID) + k
                    mean = part[:, upper * width : (upper + 1) * width] / tally[:, at : at + 1]
                    pooled[at * GRID : (at + 1) * GRID, :] = mean


def run_block(counts, ghosts, ordered, query, own_keys, own_values, side, cell_lines, faces, gain1, w_qkv, pos_proj, w_out, gain2, w_up, w_down, cells_total):
    slots = ghosts.shape[0]
    width = ordered.shape[1]
    patch = ordered.shape[0] // slots
    smem = pl.BlockSpec(memory_space=pltpu.SMEM)
    vm = pl.BlockSpec(memory_space=pltpu.VMEM)
    hbm = pl.BlockSpec(memory_space=pl.ANY)
    part = pl.BlockSpec((patch, width), lambda j: (j, 0))
    return pl.pallas_call(
        block_kernel,
        grid=(slots,),
        in_specs=[smem, smem] + [part] * 5 + [vm] + [hbm] * 4 + [vm] * 7,
        out_specs=[part, pl.BlockSpec((cells_total, width), lambda j: (0, 0))],
        out_shape=[
            jax.ShapeDtypeStruct((slots * patch, width), BF16),
            jax.ShapeDtypeStruct((cells_total, width), F32),
        ],
        scratch_shapes=[
            pltpu.VMEM((width + 16, 3 * width), BF16),
            pltpu.VMEM((2 * patch, width), BF16),
            pltpu.VMEM((2 * patch, 2 * width), BF16),
            pltpu.VMEM((slots,) + faces[0].shape, BF16),
            pltpu.VMEM((slots * patch, 2 * width), BF16),
            pltpu.SemaphoreType.DMA((slots,)),
        ],
        compiler_params=pltpu.CompilerParams(vmem_limit_bytes=VMEM_LIMIT),
        name="patch_block",
    )(counts, ghosts, ordered, query, own_keys, own_values, side, cell_lines, *faces, gain1, w_qkv, pos_proj, w_out, gain2, w_up, w_down)


def per_device(
    feats, coords, serial, cells, counts, ghosts, ln1_gain, w_qkv, pos_proj, w_out, ln2_gain, w_up, w_down
):
    rows_dev, width = feats.shape
    patch = rows_dev // ghosts.shape[0]
    slab_total = lax.axis_size("slab")
    sub_total = lax.axis_size("sub")
    cells2 = cells.reshape(1, rows_dev)
    gain1 = ln1_gain.reshape(1, width)
    near, near_aux, face0, face1, table, extra = gather_near(serial, feats, coords, cells2, 2 * patch)
    own = gather_far(serial, table, extra, near, near_aux, gain1, w_qkv, pos_proj)

    def ring(axis, size):
        up = [(i, (i + 1) % size) for i in range(size)]
        down = [(j, i) for i, j in up]
        return [lax.ppermute(face1, axis, up), lax.ppermute(face0, axis, down)]

    faces = ring("slab", slab_total) + ring("sub", sub_total)
    planes = GRID // slab_total
    lines = GRID // sub_total
    out, pooled = run_block(
        counts, ghosts, *own, faces,
        gain1, w_qkv, pos_proj, w_out, ln2_gain.reshape(1, width), w_up, w_down,
        planes * lines * GRID,
    )
    return out, pooled.reshape(planes, lines, GRID, width)


def solution(mesh):
    rows = P(("slab", "sub"))
    specs = (P(("slab", "sub"), None), P(None, ("slab", "sub")), rows, rows, rows, rows) + (P(),) * 7
    return jax.shard_map(
        per_device,
        mesh=mesh,
        in_specs=specs,
        out_specs=(P(("slab", "sub"), None), P("slab", "sub", None, None)),
        check_vma=False,
    )
```

```python
import math

import jax
import jax.numpy as jnp
from jax import lax
from jax.experimental import pallas as pl
from jax.experimental.pallas import tpu as pltpu
from jax.sharding import PartitionSpec as P

HEADS = 4
GRID = 64
EPS = 1e-05
CHUNK = 256
STEP = 256
SCALE = math.log2(math.e) / math.sqrt(32.0)
F32 = jnp.float32
BF16 = jnp.bfloat16
VMEM_LIMIT = 24 * 1024 * 1024


def dot(a, b, dims):
    return lax.dot_general(a, b, (dims, ((), ())), preferred_element_type=F32)


def normed_rows(values, gain):
    center = values - jnp.mean(values, axis=-1, keepdims=True)
    spread = jnp.mean(center * center, axis=-1, keepdims=True)
    return (center * lax.rsqrt(spread + EPS) * gain).astype(BF16)


def full_weights(w_full, w_qkv, pos_proj):
    width = w_qkv.shape[0]
    pos = pos_proj[...]
    high = pos.astype(BF16).astype(F32)
    rest = pos - high
    middle = rest.astype(BF16).astype(F32)
    low = rest - middle
    blank = jnp.zeros((16 - 9, 2 * width), F32)
    stacked = jnp.concatenate([high, middle, low, blank], axis=0).astype(BF16)
    w_full[0:width, 0 : 3 * width] = w_qkv[...]
    w_full[width : width + 16, 0 : 2 * width] = stacked
    w_full[width : width + 16, 2 * width : 3 * width] = jnp.zeros((16, width), BF16)
    if w_full.shape[0] > width + 16:
        w_full[width + 16 :, 0 : 3 * width] = jnp.zeros((width - 16, 3 * width), BF16)


def build_tables(feats, coords, cells, table, extra, lines):
    table[...] = feats[...].astype(F32)
    cell = cells[...]
    lines[0:3, :] = coords[...].astype(F32)
    lines[3:4, :] = (((cell >> 12) & 3) * 8 + ((cell >> 6) & 7)).astype(F32)
    lines[4:5, :] = (cell & 63).astype(F32)
    lines[5:6, :] = ((cell >> 13) & 1).astype(F32)
    lines[6:8, :] = jnp.zeros_like(lines[6:8, :])
    source = lax.broadcasted_iota(jnp.int32, (8, 128), 0)
    lane = lax.broadcasted_iota(jnp.int32, (8, 128), 1)
    place_spot = jnp.where((lane < 9) & (lane % 3 == source), 1.0, 0.0)
    cell_spot = jnp.where((lane == source + 6) & (source < 6), 1.0, 0.0)
    spot = jnp.where(source < 3, place_spot, cell_spot).astype(BF16)
    extra[...] = dot(lines[...].astype(BF16), spot, ((0,), (0,)))


def pick_rows(serial, first, base, table, extra, rows, more):
    for r in range(STEP):
        at = serial[first + base + r]
        rows[pl.ds(base + r, 1), :] = table[pl.ds(at, 1), :]
        more[pl.ds(base + r, 1), :] = extra[pl.ds(at, 1), :]


def make_face(face, rows, more):
    patch = rows.shape[0]
    row = lax.broadcasted_iota(jnp.int32, (16, 128), 0)
    lane = lax.broadcasted_iota(jnp.int32, (16, 128), 1)
    pick = jnp.where((row == lane) & (row < 9), 1.0, 0.0).astype(BF16)
    face[0:patch, :] = rows[...].astype(BF16)
    line = dot(pick, more[...].astype(BF16), ((1,), (1,))).astype(BF16)
    for c in range(patch // 128):
        face[patch + c * 16 : patch + c * 16 + 16, :] = line[:, c * 128 : c * 128 + 128]


def project_weights(w_full, w_qkv, pos_proj):
    width = w_qkv.shape[0]
    full_weights(w_full, w_qkv, pos_proj)
    row = lax.broadcasted_iota(jnp.int32, (width, width), 0)
    w_full[0:width, 3 * width :] = jnp.zeros((width, width), BF16)
    w_full[width:, 3 * width :] = jnp.where(row == 11, 1.0, 0.0).astype(BF16)


def project(base, offset, rows, more, gain1, w_full, outs):
    ordered, query, keys, values, side, cell_lines = outs
    width = rows.shape[1]
    row = lax.broadcasted_iota(jnp.int32, (8, 128), 0)
    lane = lax.broadcasted_iota(jnp.int32, (8, 128), 1)
    pick = jnp.where((row < 3) & (lane == row + 9), 1.0, 0.0).astype(BF16)
    wide = rows[pl.ds(base, STEP), :]
    aux = more[pl.ds(base, STEP), :].astype(BF16)
    normed = normed_rows(wide, gain1[...])
    qkv = dot(jnp.concatenate([normed, aux], axis=1), w_full[...], ((1,), (0,)))
    span = pl.ds(pl.multiple_of(base + offset, STEP), STEP)
    ordered[span, :] = wide.astype(BF16)
    query[span, :] = qkv[:, :width].astype(BF16)
    keys[span, :] = qkv[:, width : 2 * width].astype(BF16)
    values[span, :] = qkv[:, 2 * width : 3 * width].astype(BF16)
    side[span, :] = qkv[:, 3 * width :].astype(BF16)
    cell_lines[:, span] = dot(pick, aux, ((1,), (1,)))


def steps(patch, body):
    def step(block, carry):
        body(pl.multiple_of(block * STEP, STEP))
        return carry

    lax.fori_loop(0, patch // STEP, step, 0)


def first_kernel(serial_in, feats_in, coords_in, cells_in, face1, table, extra, rows1, more1, serial, feats, coords, cells, lines, sems):
    patch = rows1.shape[0]
    copies = [
        pltpu.make_async_copy(feats_in, feats, sems.at[0]),
        pltpu.make_async_copy(coords_in, coords, sems.at[1]),
        pltpu.make_async_copy(cells_in, cells, sems.at[2]),
        pltpu.make_async_copy(serial_in.at[pl.ds(patch, patch)], serial, sems.at[3]),
    ]
    for copy in copies:
        copy.start()
    for copy in copies:
        copy.wait()
    build_tables(feats, coords, cells, table, extra, lines)
    steps(patch, lambda base: pick_rows(serial, 0, base, table, extra, rows1, more1))
    make_face(face1, rows1, more1)


def second_kernel(
    serial, table, extra, rows1, more1, gain1, w_qkv, pos_proj,
    face0, ordered, query, keys, values, side, cell_lines, rows2, more2,
    w_full, rows0, more0,
):
    patch = rows1.shape[0]
    outs = (ordered, query, keys, values, side, cell_lines)
    project_weights(w_full, w_qkv, pos_proj)

    def zero(base):
        pick_rows(serial, 0, base, table, extra, rows0, more0)
        project(base, patch, rows1, more1, gain1, w_full, outs)

    def two(base):
        pick_rows(serial, 2 * patch, base, table, extra, rows2, more2)
        project(base, 0, rows0, more0, gain1, w_full, outs)

    steps(patch, zero)
    make_face(face0, rows0, more0)
    steps(patch, two)


def third_kernel(
    serial, table, extra, rows2, more2, gain1, w_qkv, pos_proj,
    near_ordered, near_query, near_keys, near_values, near_side, near_lines,
    ordered, query, keys, values, side, cell_lines,
    w_full, rows3, more3, rows4, more4,
):
    patch = rows2.shape[0]
    outs = (ordered, query, keys, values, side, cell_lines)
    project_weights(w_full, w_qkv, pos_proj)
    pairs = ((ordered, near_ordered), (query, near_query), (keys, near_keys), (values, near_values), (side, near_side))
    for far, near in pairs:
        far[0 : 2 * patch, :] = near[...]
    cell_lines[:, 0 : 2 * patch] = near_lines[...]

    def three(base):
        pick_rows(serial, 3 * patch, base, table, extra, rows3, more3)
        project(base, 2 * patch, rows2, more2, gain1, w_full, outs)

    def four(base):
        pick_rows(serial, 4 * patch, base, table, extra, rows4, more4)
        project(base, 3 * patch, rows3, more3, gain1, w_full, outs)

    steps(patch, three)
    steps(patch, four)
    steps(patch, lambda base: project(base, 4 * patch, rows4, more4, gain1, w_full, outs))


def gather_first(serial, feats, coords, cells, patch):
    total, width = feats.shape
    vm = pl.BlockSpec(memory_space=pltpu.VMEM)
    hbm = pl.BlockSpec(memory_space=pltpu.HBM)
    return pl.pallas_call(
        first_kernel,
        in_specs=[hbm] * 4,
        out_specs=[vm] * 5,
        out_shape=[
            jax.ShapeDtypeStruct((patch + patch // 8, width), BF16),
            jax.ShapeDtypeStruct((total, width), F32),
            jax.ShapeDtypeStruct((total, 128), F32),
            jax.ShapeDtypeStruct((patch, width), F32),
            jax.ShapeDtypeStruct((patch, 128), F32),
        ],
        scratch_shapes=[
            pltpu.SMEM((patch,), jnp.int32),
            pltpu.VMEM(feats.shape, BF16),
            pltpu.VMEM(coords.shape, BF16),
            pltpu.VMEM(cells.shape, jnp.int32),
            pltpu.VMEM((8, total), F32),
            pltpu.SemaphoreType.DMA((4,)),
        ],
        compiler_params=pltpu.CompilerParams(vmem_limit_bytes=VMEM_LIMIT),
        name="gather_first",
    )(*[pltpu.with_memory_space_constraint(x, pltpu.HBM) for x in (serial, feats, coords, cells)])


def row_shapes(rows, width):
    return [jax.ShapeDtypeStruct((rows, width), BF16)] * 5 + [jax.ShapeDtypeStruct((8, rows), F32)]


def gather_second(serial, table, extra, rows1, more1, gain1, w_qkv, pos_proj):
    patch, width = rows1.shape
    vm = pl.BlockSpec(memory_space=pltpu.VMEM)
    picked = [pltpu.VMEM((patch, width), F32), pltpu.VMEM((patch, 128), F32)]
    return pl.pallas_call(
        second_kernel,
        in_specs=[pl.BlockSpec(memory_space=pltpu.SMEM)] + [vm] * 7,
        out_specs=[vm] * 9,
        out_shape=[jax.ShapeDtypeStruct((patch + patch // 8, width), BF16)]
        + row_shapes(2 * patch, width)
        + [jax.ShapeDtypeStruct((patch, width), F32), jax.ShapeDtypeStruct((patch, 128), F32)],
        scratch_shapes=[pltpu.VMEM((2 * width, 4 * width), BF16)] + picked,
        compiler_params=pltpu.CompilerParams(vmem_limit_bytes=VMEM_LIMIT),
        name="gather_second",
    )(serial, table, extra, rows1, more1, gain1, w_qkv, pos_proj)


def gather_third(serial, table, extra, rows2, more2, gain1, w_qkv, pos_proj, near):
    patch, width = rows2.shape
    vm = pl.BlockSpec(memory_space=pltpu.VMEM)
    picked = [pltpu.VMEM((patch, width), F32), pltpu.VMEM((patch, 128), F32)]
    return pl.pallas_call(
        third_kernel,
        in_specs=[pl.BlockSpec(memory_space=pltpu.SMEM)] + [vm] * 13,
        out_specs=[vm] * 6,
        out_shape=row_shapes(table.shape[0], width),
        scratch_shapes=[pltpu.VMEM((2 * width, 4 * width), BF16)] + picked * 2,
        compiler_params=pltpu.CompilerParams(vmem_limit_bytes=VMEM_LIMIT),
        name="gather_third",
    )(serial, table, extra, rows2, more2, gain1, w_qkv, pos_proj, *near)


def block_kernel(
    counts, ghosts, ordered, query, own_keys, own_values, side, cell_lines, face1, face2, face3, face4,
    gain1, w_qkv, pos_proj, w_out, gain2, w_up, w_down,
    out, pooled,
    w_full, keys, values, faces, rows_all, sems,
):
    slot = pl.program_id(0)
    patch, width = out.shape
    slots = ghosts.shape[0]
    depth = width // HEADS
    sources = (face1, face2, face3, face4)

    @pl.when(slot == 0)
    def start():
        for j in range(slots):
            for g in range(4):
                @pl.when((j < counts[0]) & (ghosts[j] == g + 1))
                def fetch():
                    pltpu.make_async_copy(sources[g], faces.at[j], sems.at[j]).start()
        full_weights(w_full, w_qkv, pos_proj)
        values[:, width:] = jnp.ones((2 * patch, width), BF16)

    live = slot < counts[0]
    base = pl.multiple_of(slot * patch, patch)

    @pl.when(jnp.logical_not(live))
    def dead():
        out[...] = jnp.zeros_like(out)
        rows_all[pl.ds(base, patch), :] = jnp.zeros((patch, 2 * width), BF16)

    def finish(lower, mixed):
        stream = (
            ordered[lower : lower + CHUNK, :].astype(F32) + dot(mixed.astype(BF16), w_out[...], ((1,), (0,)))
        ).astype(BF16)
        yield
        wide = stream.astype(F32)
        normed2 = normed_rows(wide, gain2[...])
        yield
        inner = jax.nn.gelu(dot(normed2, w_up[...], ((1,), (0,)))).astype(BF16)
        yield
        result = (wide + dot(inner, w_down[...], ((1,), (0,)))).astype(BF16)
        out[lower : lower + CHUNK, :] = result
        upper = side[lower : lower + CHUNK, :] > 0.5
        none = jnp.zeros_like(result)
        rows_all[pl.ds(base + lower, CHUNK), 0:width] = jnp.where(upper, none, result)
        rows_all[pl.ds(base + lower, CHUNK), width:] = jnp.where(upper, result, none)
        yield

    def attend(count):
        lane = lax.broadcasted_iota(jnp.int32, (CHUNK, width), 1)

        def head_scores(unit):
            lower = unit // HEADS * CHUNK
            h = unit % HEADS
            mine = (lane >= h * depth) & (lane < (h + 1) * depth)
            q = query[lower : lower + CHUNK, :]
            return mine, dot(jnp.where(mine, q, jnp.zeros_like(q)), keys[0:count, :], ((1,), (1,)))

        units = patch // CHUNK * HEADS
        tail = iter(())
        ahead = head_scores(0)
        mixed = jnp.zeros((CHUNK, width), F32)
        for unit in range(units):
            mine, scores = ahead
            if unit + 1 < units:
                ahead = head_scores(unit + 1)
            next(tail, None)
            top = jnp.max(scores, axis=-1, keepdims=True)
            weights = jnp.exp2((scores - top) * SCALE).astype(BF16)
            summed = dot(weights, values[0:count, :], ((1,), (0,)))
            mixed = jnp.where(mine, summed[:, :width] / summed[:, width:], mixed)
            if unit % HEADS == HEADS - 1:
                tail = finish(unit // HEADS * CHUNK, mixed)
        for _ in tail:
            pass

    @pl.when(live)
    def work():
        keys[0:patch, :] = own_keys[...]
        values[0:patch, 0:width] = own_values[...]
        ghost = ghosts[slot]

        @pl.when(ghost > 0)
        def with_ghost():
            pltpu.make_async_copy(face1, faces.at[slot], sems.at[slot]).wait()
            there = normed_rows(faces[slot, 0:patch, :].astype(F32), gain1[...])
            line = jnp.concatenate(
                [faces[slot, patch + c * 16 : patch + c * 16 + 16, :] for c in range(patch // 128)],
                axis=1,
            )
            slab_no = lax.axis_index("slab")
            sub_no = lax.axis_index("sub")
            on_x = ghost < 3
            down = (ghost == 1) | (ghost == 3)
            place = jnp.where(on_x, slab_no, sub_no)
            edge = jnp.where(down, 0, jnp.where(on_x, lax.axis_size("slab"), lax.axis_size("sub")) - 1)
            amount = jnp.where(place == edge, jnp.where(down, -1.0, 1.0), 0.0)
            bump = jnp.where(on_x, pos_proj[0:1, width:], pos_proj[1:2, width:]) * amount
            both = dot(there, w_full[0:width, width:], ((1,), (0,)))
            lifted = dot(line, w_full[width : width + 16, width : 2 * width], ((0,), (0,)))
            keys[patch:, :] = (both[:, :width] + (lifted + bump)).astype(BF16)
            values[patch:, 0:width] = both[:, width:].astype(BF16)
            attend(2 * patch)

        @pl.when(ghost == 0)
        def without_ghost():
            attend(patch)

    @pl.when(slot == slots - 1)
    def pool():
        half = pooled.shape[0] // 2
        row_no = lax.broadcasted_iota(jnp.int32, (1, slots * patch), 1)
        column = jnp.where(row_no < counts[0] * patch, cell_lines[0:1, :], -1.0)
        depth_no = cell_lines[1:2, :]
        ids = lax.broadcasted_iota(jnp.int32, (GRID, 1), 0).astype(F32)
        by_column = jnp.where(column == ids[0 : 2 * half // GRID], 1.0, 0.0).astype(BF16)
        by_depth = jnp.where(depth_no == ids, 1.0, 0.0).astype(BF16)
        tally = jnp.maximum(dot(by_depth, by_column, ((1,), (1,))), 1.0)
        lower_cell = (column - cell_lines[2:3, :] * (half // GRID)) * GRID + depth_no
        wide_ids = lax.broadcasted_iota(jnp.int32, (256, 1), 0).astype(F32)
        for c in range(half // 256):
            onehot = jnp.where(lower_cell == wide_ids + c * 256.0, 1.0, 0.0).astype(BF16)
            summed = dot(onehot, rows_all[...], ((1,), (0,)))
            for k in range(256 // GRID):
                part = summed[k * GRID : (k + 1) * GRID]
                for upper in range(2):
                    at = upper * (half // GRID) + c * (256 // GRID) + k
                    mean = part[:, upper * width : (upper + 1) * width] / tally[:, at : at + 1]
                    pooled[at * GRID : (at + 1) * GRID, :] = mean


def run_block(counts, ghosts, ordered, query, own_keys, own_values, side, cell_lines, faces, gain1, w_qkv, pos_proj, w_out, gain2, w_up, w_down, cells_total):
    slots = ghosts.shape[0]
    width = ordered.shape[1]
    patch = ordered.shape[0] // slots
    smem = pl.BlockSpec(memory_space=pltpu.SMEM)
    vm = pl.BlockSpec(memory_space=pltpu.VMEM)
    hbm = pl.BlockSpec(memory_space=pl.ANY)
    part = pl.BlockSpec((patch, width), lambda j: (j, 0))
    return pl.pallas_call(
        block_kernel,
        grid=(slots,),
        in_specs=[smem, smem] + [part] * 5 + [vm] + [hbm] * 4 + [vm] * 7,
        out_specs=[part, pl.BlockSpec((cells_total, width), lambda j: (0, 0))],
        out_shape=[
            jax.ShapeDtypeStruct((slots * patch, width), BF16),
            jax.ShapeDtypeStruct((cells_total, width), F32),
        ],
        scratch_shapes=[
            pltpu.VMEM((width + 16, 3 * width), BF16),
            pltpu.VMEM((2 * patch, width), BF16),
            pltpu.VMEM((2 * patch, 2 * width), BF16),
            pltpu.VMEM((slots,) + faces[0].shape, BF16),
            pltpu.VMEM((slots * patch, 2 * width), BF16),
            pltpu.SemaphoreType.DMA((slots,)),
        ],
        compiler_params=pltpu.CompilerParams(vmem_limit_bytes=VMEM_LIMIT),
        name="patch_block",
    )(counts, ghosts, ordered, query, own_keys, own_values, side, cell_lines, *faces, gain1, w_qkv, pos_proj, w_out, gain2, w_up, w_down)


def send(face, shift):
    received = []
    for axis in ("sub", "slab"):
        size = lax.axis_size(axis)
        received.append(lax.ppermute(face, axis, [(i, (i + shift) % size) for i in range(size)]))
    return received[1], received[0]


def per_device(
    feats, coords, serial, cells, counts, ghosts, ln1_gain, w_qkv, pos_proj, w_out, ln2_gain, w_up, w_down
):
    rows_dev, width = feats.shape
    patch = rows_dev // ghosts.shape[0]
    slab_total = lax.axis_size("slab")
    sub_total = lax.axis_size("sub")
    cells2 = cells.reshape(1, rows_dev)
    gain1 = ln1_gain.reshape(1, width)
    face1, table, extra, rows1, more1 = gather_first(serial, feats, coords, cells2, patch)
    below = send(face1, 1)
    face0, *near, rows2, more2 = gather_second(serial, table, extra, rows1, more1, gain1, w_qkv, pos_proj)
    above = send(face0, -1)
    own = gather_third(serial, table, extra, rows2, more2, gain1, w_qkv, pos_proj, near)
    faces = [below[0], above[0], below[1], above[1]]

    planes = GRID // slab_total
    lines = GRID // sub_total
    out, pooled = run_block(
        counts, ghosts, *own, faces,
        gain1, w_qkv, pos_proj, w_out, ln2_gain.reshape(1, width), w_up, w_down,
        planes * lines * GRID,
    )
    return out, pooled.reshape(planes, lines, GRID, width)


def solution(mesh):
    rows = P(("slab", "sub"))
    specs = (P(("slab", "sub"), None), P(None, ("slab", "sub")), rows, rows, rows, rows) + (P(),) * 7
    return jax.shard_map(
        per_device,
        mesh=mesh,
        in_specs=specs,
        out_specs=(P(("slab", "sub"), None), P("slab", "sub", None, None)),
        check_vma=False,
    )
```

```python
import functools
import math

import jax
import jax.numpy as jnp
from jax import lax
from jax.experimental import pallas as pl
from jax.experimental.pallas import tpu as pltpu
from jax.sharding import PartitionSpec as P

HEADS = 4
GRID = 64
EPS = 1e-05
CHUNK = 256
STEP = 256
PREPARE_FROM = 0
SCALE = math.log2(math.e) / math.sqrt(32.0)
F32 = jnp.float32
BF16 = jnp.bfloat16
VMEM_LIMIT = 24 * 1024 * 1024


def dot(a, b, dims):
    return lax.dot_general(a, b, (dims, ((), ())), preferred_element_type=F32)


def normed_rows(values, gain):
    center = values - jnp.mean(values, axis=-1, keepdims=True)
    spread = jnp.mean(center * center, axis=-1, keepdims=True)
    return (center * lax.rsqrt(spread + EPS) * gain).astype(BF16)


def full_weights(w_full, w_qkv, pos_proj):
    width = w_qkv.shape[0]
    pos = pos_proj[...]
    high = pos.astype(BF16).astype(F32)
    rest = pos - high
    middle = rest.astype(BF16).astype(F32)
    low = rest - middle
    blank = jnp.zeros((16 - 9, 2 * width), F32)
    stacked = jnp.concatenate([high, middle, low, blank], axis=0).astype(BF16)
    w_full[0:width, 0 : 3 * width] = w_qkv[...]
    w_full[width : width + 16, 0 : 2 * width] = stacked
    w_full[width : width + 16, 2 * width : 3 * width] = jnp.zeros((16, width), BF16)
    if w_full.shape[0] > width + 16:
        w_full[width + 16 :, 0 : 3 * width] = jnp.zeros((width - 16, 3 * width), BF16)


def build_tables(feats, coords, cells, table, extra, lines):
    table[...] = feats[...].astype(F32)
    cell = cells[...]
    lines[0:3, :] = coords[...].astype(F32)
    lines[3:4, :] = (((cell >> 12) & 3) * 8 + ((cell >> 6) & 7)).astype(F32)
    lines[4:5, :] = (cell & 63).astype(F32)
    lines[5:6, :] = ((cell >> 13) & 1).astype(F32)
    lines[6:8, :] = jnp.zeros_like(lines[6:8, :])
    source = lax.broadcasted_iota(jnp.int32, (8, 128), 0)
    lane = lax.broadcasted_iota(jnp.int32, (8, 128), 1)
    place_spot = jnp.where((lane < 9) & (lane % 3 == source), 1.0, 0.0)
    cell_spot = jnp.where((lane == source + 6) & (source < 6), 1.0, 0.0)
    spot = jnp.where(source < 3, place_spot, cell_spot).astype(BF16)
    extra[...] = dot(lines[...].astype(BF16), spot, ((0,), (0,)))


def pick_rows(serial, first, base, table, extra, rows, more):
    for r in range(STEP):
        at = serial[first + base + r]
        rows[pl.ds(base + r, 1), :] = table[pl.ds(at, 1), :]
        more[pl.ds(base + r, 1), :] = extra[pl.ds(at, 1), :]


def make_face(face, rows, more):
    patch = rows.shape[0]
    row = lax.broadcasted_iota(jnp.int32, (16, 128), 0)
    lane = lax.broadcasted_iota(jnp.int32, (16, 128), 1)
    pick = jnp.where((row == lane) & (row < 9), 1.0, 0.0).astype(BF16)
    face[0:patch, :] = rows[...].astype(BF16)
    line = dot(pick, more[...].astype(BF16), ((1,), (1,))).astype(BF16)
    for c in range(patch // 128):
        face[patch + c * 16 : patch + c * 16 + 16, :] = line[:, c * 128 : c * 128 + 128]


def project_weights(w_full, w_qkv, pos_proj):
    width = w_qkv.shape[0]
    full_weights(w_full, w_qkv, pos_proj)
    row = lax.broadcasted_iota(jnp.int32, (width, width), 0)
    w_full[0:width, 3 * width :] = jnp.zeros((width, width), BF16)
    w_full[width:, 3 * width :] = jnp.where(row == 11, 1.0, 0.0).astype(BF16)


def project(base, offset, rows, more, gain1, w_full, outs):
    ordered, query, keys, values, side, cell_lines = outs
    width = rows.shape[1]
    row = lax.broadcasted_iota(jnp.int32, (8, 128), 0)
    lane = lax.broadcasted_iota(jnp.int32, (8, 128), 1)
    pick = jnp.where((row < 3) & (lane == row + 9), 1.0, 0.0).astype(BF16)
    wide = rows[pl.ds(base, STEP), :]
    aux = more[pl.ds(base, STEP), :].astype(BF16)
    normed = normed_rows(wide, gain1[...])
    qkv = dot(jnp.concatenate([normed, aux], axis=1), w_full[...], ((1,), (0,)))
    span = pl.ds(pl.multiple_of(base + offset, STEP), STEP)
    ordered[span, :] = wide.astype(BF16)
    query[span, :] = qkv[:, :width].astype(BF16)
    keys[span, :] = qkv[:, width : 2 * width].astype(BF16)
    values[span, :] = qkv[:, 2 * width : 3 * width].astype(BF16)
    side[span, :] = qkv[:, 3 * width :].astype(BF16)
    cell_lines[:, span] = dot(pick, aux, ((1,), (1,)))


def steps(patch, body):
    def step(block, carry):
        body(pl.multiple_of(block * STEP, STEP))
        return carry

    lax.fori_loop(0, patch // STEP, step, 0)


def first_kernel(
    serial_in, feats_in, coords_in, cells_in,
    face0, face1, table, extra, rows0, more0, rows1, more1,
    serial, feats, coords, cells, lines, sems,
):
    patch = rows1.shape[0]
    copies = [
        pltpu.make_async_copy(feats_in, feats, sems.at[0]),
        pltpu.make_async_copy(coords_in, coords, sems.at[1]),
        pltpu.make_async_copy(cells_in, cells, sems.at[2]),
        pltpu.make_async_copy(serial_in.at[pl.ds(0, 2 * patch)], serial, sems.at[3]),
    ]
    for copy in copies:
        copy.start()
    for copy in copies:
        copy.wait()
    build_tables(feats, coords, cells, table, extra, lines)
    steps(patch, lambda base: pick_rows(serial, 0, base, table, extra, rows0, more0))
    make_face(face0, rows0, more0)
    steps(patch, lambda base: pick_rows(serial, patch, base, table, extra, rows1, more1))
    make_face(face1, rows1, more1)


def second_kernel(
    serial, table, extra, rows0, more0, rows1, more1, gain1, w_qkv, pos_proj,
    ordered, query, keys, values, side, cell_lines,
    w_full, rows2, more2, rows3, more3, rows4, more4,
):
    patch = rows1.shape[0]
    outs = (ordered, query, keys, values, side, cell_lines)
    picked = ((rows0, more0), (rows1, more1), (rows2, more2), (rows3, more3), (rows4, more4))
    project_weights(w_full, w_qkv, pos_proj)
    for slot in range(len(picked)):
        def both(base):
            if slot + 2 < len(picked):
                pick_rows(serial, (slot + 2) * patch, base, table, extra, *picked[slot + 2])
            project(base, slot * patch, *picked[slot], gain1, w_full, outs)

        steps(patch, both)


def gather_first(serial, feats, coords, cells, patch):
    total, width = feats.shape
    vm = pl.BlockSpec(memory_space=pltpu.VMEM)
    hbm = pl.BlockSpec(memory_space=pltpu.HBM)
    picked = [jax.ShapeDtypeStruct((patch, width), F32), jax.ShapeDtypeStruct((patch, 128), F32)]
    return pl.pallas_call(
        first_kernel,
        in_specs=[hbm] * 4,
        out_specs=[vm] * 8,
        out_shape=[jax.ShapeDtypeStruct((patch + patch // 8, width), BF16)] * 2
        + [jax.ShapeDtypeStruct((total, width), F32), jax.ShapeDtypeStruct((total, 128), F32)]
        + picked * 2,
        scratch_shapes=[
            pltpu.SMEM((2 * patch,), jnp.int32),
            pltpu.VMEM(feats.shape, BF16),
            pltpu.VMEM(coords.shape, BF16),
            pltpu.VMEM(cells.shape, jnp.int32),
            pltpu.VMEM((8, total), F32),
            pltpu.SemaphoreType.DMA((4,)),
        ],
        compiler_params=pltpu.CompilerParams(vmem_limit_bytes=VMEM_LIMIT),
        name="gather_first",
    )(*[pltpu.with_memory_space_constraint(x, pltpu.HBM) for x in (serial, feats, coords, cells)])


def gather_second(serial, table, extra, picked, gain1, w_qkv, pos_proj):
    patch, width = picked[0].shape
    total = table.shape[0]
    vm = pl.BlockSpec(memory_space=pltpu.VMEM)
    return pl.pallas_call(
        second_kernel,
        in_specs=[pl.BlockSpec(memory_space=pltpu.SMEM)] + [vm] * 9,
        out_specs=[vm] * 6,
        out_shape=[jax.ShapeDtypeStruct((total, width), BF16)] * 5 + [jax.ShapeDtypeStruct((8, total), F32)],
        scratch_shapes=[pltpu.VMEM((2 * width, 4 * width), BF16)]
        + [pltpu.VMEM((patch, width), F32), pltpu.VMEM((patch, 128), F32)] * 3,
        compiler_params=pltpu.CompilerParams(vmem_limit_bytes=VMEM_LIMIT),
        name="gather_second",
    )(serial, table, extra, *picked, gain1, w_qkv, pos_proj)


def block_kernel(
    counts, ghosts, ordered, query, own_keys, own_values, side, cell_lines, face1, face2, face3, face4,
    gain1, w_qkv, pos_proj, w_out, gain2, w_up, w_down,
    out, pooled,
    w_full, keys, values, next_keys, next_values, faces, rows_all, sems,
):
    slot = pl.program_id(0)
    patch, width = out.shape
    slots = ghosts.shape[0]
    depth = width // HEADS
    sources = (face1, face2, face3, face4)

    @pl.when(slot == 0)
    def start():
        for j in range(slots):
            for g in range(4):
                @pl.when((j < counts[0]) & (ghosts[j] == g + 1))
                def fetch():
                    pltpu.make_async_copy(sources[g], faces.at[j], sems.at[j]).start()
        full_weights(w_full, w_qkv, pos_proj)
        values[:, width:] = jnp.ones((2 * patch, width), BF16)

    def arrive(slot_no):
        @pl.when((slot_no < counts[0]) & (ghosts[jnp.minimum(slot_no, slots - 1)] > 0))
        def wait():
            pltpu.make_async_copy(face1, faces.at[jnp.minimum(slot_no, slots - 1)], sems.at[jnp.minimum(slot_no, slots - 1)]).wait()

    def prepare(slot_no):
        ghost = ghosts[slot_no]
        slab_no = lax.axis_index("slab")
        sub_no = lax.axis_index("sub")
        on_x = ghost < 3
        down = (ghost == 1) | (ghost == 3)
        place = jnp.where(on_x, slab_no, sub_no)
        edge = jnp.where(down, 0, jnp.where(on_x, lax.axis_size("slab"), lax.axis_size("sub")) - 1)
        amount = jnp.where(place == edge, jnp.where(down, -1.0, 1.0), 0.0)
        bump = jnp.where(on_x, pos_proj[0:1, width:], pos_proj[1:2, width:]) * amount
        for lower in range(0, patch, CHUNK):
            there = normed_rows(faces[slot_no, lower : lower + CHUNK, :].astype(F32), gain1[...])
            yield
            first = patch + lower // 8
            line = jnp.concatenate(
                [faces[slot_no, first + c * 16 : first + c * 16 + 16, :] for c in range(CHUNK // 128)],
                axis=1,
            )
            both = dot(there, w_full[0:width, width:], ((1,), (0,)))
            lifted = dot(line, w_full[width : width + 16, width : 2 * width], ((0,), (0,)))
            next_keys[lower : lower + CHUNK, :] = (both[:, :width] + (lifted + bump)).astype(BF16)
            next_values[lower : lower + CHUNK, :] = both[:, width:].astype(BF16)
            yield

    @pl.when(slot == 0)
    def prime():
        arrive(0)
        for _ in prepare(0):
            pass

    live = slot < counts[0]
    base = pl.multiple_of(slot * patch, patch)

    @pl.when(jnp.logical_not(live))
    def dead():
        out[...] = jnp.zeros_like(out)
        rows_all[pl.ds(base, patch), :] = jnp.zeros((patch, 2 * width), BF16)

    def finish(lower, mixed):
        stream = (
            ordered[lower : lower + CHUNK, :].astype(F32) + dot(mixed.astype(BF16), w_out[...], ((1,), (0,)))
        ).astype(BF16)
        yield
        wide = stream.astype(F32)
        normed2 = normed_rows(wide, gain2[...])
        yield
        inner = jax.nn.gelu(dot(normed2, w_up[...], ((1,), (0,)))).astype(BF16)
        yield
        result = (wide + dot(inner, w_down[...], ((1,), (0,)))).astype(BF16)
        out[lower : lower + CHUNK, :] = result
        upper = side[lower : lower + CHUNK, :] > 0.5
        none = jnp.zeros_like(result)
        rows_all[pl.ds(base + lower, CHUNK), 0:width] = jnp.where(upper, none, result)
        rows_all[pl.ds(base + lower, CHUNK), width:] = jnp.where(upper, result, none)
        yield

    def attend(count):
        lane = lax.broadcasted_iota(jnp.int32, (CHUNK, width), 1)

        def head_scores(unit):
            lower = unit // HEADS * CHUNK
            h = unit % HEADS
            mine = (lane >= h * depth) & (lane < (h + 1) * depth)
            q = query[lower : lower + CHUNK, :]
            return mine, dot(jnp.where(mine, q, jnp.zeros_like(q)), keys[0:count, :], ((1,), (1,)))

        units = patch // CHUNK * HEADS
        tail = iter(())
        ahead_of = prepare(jnp.minimum(slot + 1, slots - 1))
        ahead = head_scores(0)
        mixed = jnp.zeros((CHUNK, width), F32)
        for unit in range(units):
            mine, scores = ahead
            if unit + 1 < units:
                ahead = head_scores(unit + 1)
            next(tail, None)
            if unit >= PREPARE_FROM:
                next(ahead_of, None)
            top = jnp.max(scores, axis=-1, keepdims=True)
            weights = jnp.exp2((scores - top) * SCALE).astype(BF16)
            summed = dot(weights, values[0:count, :], ((1,), (0,)))
            mixed = jnp.where(mine, summed[:, :width] / summed[:, width:], mixed)
            if unit % HEADS == HEADS - 1:
                tail = finish(unit // HEADS * CHUNK, mixed)
        for _ in tail:
            pass
        for _ in ahead_of:
            pass

    @pl.when(live)
    def work():
        keys[0:patch, :] = own_keys[...]
        values[0:patch, 0:width] = own_values[...]
        ghost = ghosts[slot]
        arrive(slot + 1)

        @pl.when(ghost > 0)
        def with_ghost():
            keys[patch:, :] = next_keys[...]
            values[patch:, 0:width] = next_values[...]
            attend(2 * patch)

        @pl.when(ghost == 0)
        def without_ghost():
            attend(patch)

    @pl.when(slot == slots - 1)
    def pool():
        half = pooled.shape[0] // 2
        row_no = lax.broadcasted_iota(jnp.int32, (1, slots * patch), 1)
        column = jnp.where(row_no < counts[0] * patch, cell_lines[0:1, :], -1.0)
        depth_no = cell_lines[1:2, :]
        ids = lax.broadcasted_iota(jnp.int32, (GRID, 1), 0).astype(F32)
        by_column = jnp.where(column == ids[0 : 2 * half // GRID], 1.0, 0.0).astype(BF16)
        by_depth = jnp.where(depth_no == ids, 1.0, 0.0).astype(BF16)
        tally = jnp.maximum(dot(by_depth, by_column, ((1,), (1,))), 1.0)
        lower_cell = (column - cell_lines[2:3, :] * (half // GRID)) * GRID + depth_no
        wide_ids = lax.broadcasted_iota(jnp.int32, (256, 1), 0).astype(F32)
        for c in range(half // 256):
            onehot = jnp.where(lower_cell == wide_ids + c * 256.0, 1.0, 0.0).astype(BF16)
            summed = dot(onehot, rows_all[...], ((1,), (0,)))
            for k in range(256 // GRID):
                part = summed[k * GRID : (k + 1) * GRID]
                for upper in range(2):
                    at = upper * (half // GRID) + c * (256 // GRID) + k
                    mean = part[:, upper * width : (upper + 1) * width] / tally[:, at : at + 1]
                    pooled[at * GRID : (at + 1) * GRID, :] = mean


def run_block(counts, ghosts, ordered, query, own_keys, own_values, side, cell_lines, faces, gain1, w_qkv, pos_proj, w_out, gain2, w_up, w_down, cells_total):
    slots = ghosts.shape[0]
    width = ordered.shape[1]
    patch = ordered.shape[0] // slots
    smem = pl.BlockSpec(memory_space=pltpu.SMEM)
    vm = pl.BlockSpec(memory_space=pltpu.VMEM)
    hbm = pl.BlockSpec(memory_space=pl.ANY)
    part = pl.BlockSpec((patch, width), lambda j: (j, 0))
    return pl.pallas_call(
        block_kernel,
        grid=(slots,),
        in_specs=[smem, smem] + [part] * 5 + [vm] + [hbm] * 4 + [vm] * 7,
        out_specs=[part, pl.BlockSpec((cells_total, width), lambda j: (0, 0))],
        out_shape=[
            jax.ShapeDtypeStruct((slots * patch, width), BF16),
            jax.ShapeDtypeStruct((cells_total, width), F32),
        ],
        scratch_shapes=[
            pltpu.VMEM((width + 16, 3 * width), BF16),
            pltpu.VMEM((2 * patch, width), BF16),
            pltpu.VMEM((2 * patch, 2 * width), BF16),
            pltpu.VMEM((patch, width), BF16),
            pltpu.VMEM((patch, width), BF16),
            pltpu.VMEM((slots,) + faces[0].shape, BF16),
            pltpu.VMEM((slots * patch, 2 * width), BF16),
            pltpu.SemaphoreType.DMA((slots,)),
        ],
        compiler_params=pltpu.CompilerParams(vmem_limit_bytes=VMEM_LIMIT),
        name="patch_block",
    )(counts, ghosts, ordered, query, own_keys, own_values, side, cell_lines, *faces, gain1, w_qkv, pos_proj, w_out, gain2, w_up, w_down)


def send(face, shift):
    received = []
    for axis in ("slab", "sub"):
        size = lax.axis_size(axis)
        received.append(lax.ppermute(face, axis, [(i, (i + shift) % size) for i in range(size)]))
    return received


def per_device(
    feats, coords, serial, cells, counts, ghosts, ln1_gain, w_qkv, pos_proj, w_out, ln2_gain, w_up, w_down
):
    rows_dev, width = feats.shape
    patch = rows_dev // ghosts.shape[0]
    slab_total = lax.axis_size("slab")
    sub_total = lax.axis_size("sub")
    cells2 = cells.reshape(1, rows_dev)
    gain1 = ln1_gain.reshape(1, width)
    face0, face1, table, extra, *picked = gather_first(serial, feats, coords, cells2, patch)
    own = gather_second(serial, table, extra, picked, gain1, w_qkv, pos_proj)
    below = send(face1, 1)
    above = send(face0, -1)
    faces = [below[0], above[0], below[1], above[1]]

    planes = GRID // slab_total
    lines = GRID // sub_total
    out, pooled = run_block(
        counts, ghosts, *own, faces,
        gain1, w_qkv, pos_proj, w_out, ln2_gain.reshape(1, width), w_up, w_down,
        planes * lines * GRID,
    )
    return out, pooled.reshape(planes, lines, GRID, width)


def solution(mesh):
    rows = P(("slab", "sub"))
    specs = (P(("slab", "sub"), None), P(None, ("slab", "sub")), rows, rows, rows, rows) + (P(),) * 7
    return jax.shard_map(
        per_device,
        mesh=mesh,
        in_specs=specs,
        out_specs=(P(("slab", "sub"), None), P("slab", "sub", None, None)),
        check_vma=False,
    )
```

```python
import functools
import math

import jax
import jax.numpy as jnp
from jax import lax
from jax.experimental import pallas as pl
from jax.experimental.pallas import tpu as pltpu
from jax.sharding import PartitionSpec as P

HEADS = 4
GRID = 64
EPS = 1e-05
CHUNK = 256
STEP = 1024
PREPARE_FROM = 0
SCALE = math.log2(math.e) / math.sqrt(32.0)
F32 = jnp.float32
BF16 = jnp.bfloat16
VMEM_LIMIT = 24 * 1024 * 1024


def dot(a, b, dims):
    return lax.dot_general(a, b, (dims, ((), ())), preferred_element_type=F32)


def normed_rows(values, gain):
    center = values - jnp.mean(values, axis=-1, keepdims=True)
    spread = jnp.mean(center * center, axis=-1, keepdims=True)
    return (center * lax.rsqrt(spread + EPS) * gain).astype(BF16)


def full_weights(w_full, w_qkv, pos_proj):
    width = w_qkv.shape[0]
    pos = pos_proj[...]
    high = pos.astype(BF16).astype(F32)
    rest = pos - high
    middle = rest.astype(BF16).astype(F32)
    low = rest - middle
    blank = jnp.zeros((16 - 9, 2 * width), F32)
    stacked = jnp.concatenate([high, middle, low, blank], axis=0).astype(BF16)
    w_full[0:width, 0 : 3 * width] = w_qkv[...]
    w_full[width : width + 16, 0 : 2 * width] = stacked
    w_full[width : width + 16, 2 * width : 3 * width] = jnp.zeros((16, width), BF16)
    if w_full.shape[0] > width + 16:
        w_full[width + 16 :, 0 : 3 * width] = jnp.zeros((width - 16, 3 * width), BF16)


def build_tables(feats, coords, cells, table, extra, lines):
    table[...] = feats[...].astype(F32)
    cell = cells[...]
    lines[0:3, :] = coords[...].astype(F32)
    lines[3:4, :] = (((cell >> 12) & 3) * 8 + ((cell >> 6) & 7)).astype(F32)
    lines[4:5, :] = (cell & 63).astype(F32)
    lines[5:6, :] = ((cell >> 13) & 1).astype(F32)
    lines[6:8, :] = jnp.zeros_like(lines[6:8, :])
    source = lax.broadcasted_iota(jnp.int32, (8, 128), 0)
    lane = lax.broadcasted_iota(jnp.int32, (8, 128), 1)
    place_spot = jnp.where((lane < 9) & (lane % 3 == source), 1.0, 0.0)
    cell_spot = jnp.where((lane == source + 6) & (source < 6), 1.0, 0.0)
    spot = jnp.where(source < 3, place_spot, cell_spot).astype(BF16)
    extra[...] = dot(lines[...].astype(BF16), spot, ((0,), (0,)))


def pick_rows(serial, first, base, table, extra, rows, more):
    for r in range(STEP):
        at = serial[first + base + r]
        rows[pl.ds(base + r, 1), :] = table[pl.ds(at, 1), :]
        more[pl.ds(base + r, 1), :] = extra[pl.ds(at, 1), :]


def make_face(face, rows, more):
    patch = rows.shape[0]
    row = lax.broadcasted_iota(jnp.int32, (16, 128), 0)
    lane = lax.broadcasted_iota(jnp.int32, (16, 128), 1)
    pick = jnp.where((row == lane) & (row < 9), 1.0, 0.0).astype(BF16)
    face[0:patch, :] = rows[...].astype(BF16)
    line = dot(pick, more[...].astype(BF16), ((1,), (1,))).astype(BF16)
    for c in range(patch // 128):
        face[patch + c * 16 : patch + c * 16 + 16, :] = line[:, c * 128 : c * 128 + 128]


def project_weights(w_full, w_qkv, pos_proj):
    width = w_qkv.shape[0]
    full_weights(w_full, w_qkv, pos_proj)
    row = lax.broadcasted_iota(jnp.int32, (width, width), 0)
    w_full[0:width, 3 * width :] = jnp.zeros((width, width), BF16)
    w_full[width:, 3 * width :] = jnp.where(row == 11, 1.0, 0.0).astype(BF16)


def project(base, offset, rows, more, gain1, w_full, outs):
    ordered, query, keys, values, side, cell_lines = outs
    width = rows.shape[1]
    row = lax.broadcasted_iota(jnp.int32, (8, 128), 0)
    lane = lax.broadcasted_iota(jnp.int32, (8, 128), 1)
    pick = jnp.where((row < 3) & (lane == row + 9), 1.0, 0.0).astype(BF16)
    wide = rows[pl.ds(base, STEP), :]
    aux = more[pl.ds(base, STEP), :].astype(BF16)
    normed = normed_rows(wide, gain1[...])
    qkv = dot(jnp.concatenate([normed, aux], axis=1), w_full[...], ((1,), (0,)))
    span = pl.ds(pl.multiple_of(base + offset, STEP), STEP)
    ordered[span, :] = wide.astype(BF16)
    query[span, :] = qkv[:, :width].astype(BF16)
    keys[span, :] = qkv[:, width : 2 * width].astype(BF16)
    values[span, :] = qkv[:, 2 * width : 3 * width].astype(BF16)
    side[span, :] = qkv[:, 3 * width :].astype(BF16)
    cell_lines[:, span] = dot(pick, aux, ((1,), (1,)))


def steps(patch, body):
    def step(block, carry):
        body(pl.multiple_of(block * STEP, STEP))
        return carry

    lax.fori_loop(0, patch // STEP, step, 0)


def first_kernel(
    serial_in, feats_in, coords_in, cells_in,
    face0, face1, table, extra, rows0, more0, rows1, more1,
    serial, feats, coords, cells, lines, sems,
):
    patch = rows1.shape[0]
    copies = [
        pltpu.make_async_copy(feats_in, feats, sems.at[0]),
        pltpu.make_async_copy(coords_in, coords, sems.at[1]),
        pltpu.make_async_copy(cells_in, cells, sems.at[2]),
        pltpu.make_async_copy(serial_in.at[pl.ds(0, 2 * patch)], serial, sems.at[3]),
    ]
    for copy in copies:
        copy.start()
    for copy in copies:
        copy.wait()
    build_tables(feats, coords, cells, table, extra, lines)
    steps(patch, lambda base: pick_rows(serial, 0, base, table, extra, rows0, more0))
    make_face(face0, rows0, more0)
    steps(patch, lambda base: pick_rows(serial, patch, base, table, extra, rows1, more1))
    make_face(face1, rows1, more1)


def second_kernel(
    serial, table, extra, rows0, more0, rows1, more1, gain1, w_qkv, pos_proj,
    ordered, query, keys, values, side, cell_lines,
    w_full, rows2, more2, rows3, more3, rows4, more4,
):
    patch = rows1.shape[0]
    outs = (ordered, query, keys, values, side, cell_lines)
    picked = ((rows0, more0), (rows1, more1), (rows2, more2), (rows3, more3), (rows4, more4))
    project_weights(w_full, w_qkv, pos_proj)
    for slot in range(len(picked)):
        def both(base):
            if slot + 2 < len(picked):
                pick_rows(serial, (slot + 2) * patch, base, table, extra, *picked[slot + 2])
            project(base, slot * patch, *picked[slot], gain1, w_full, outs)

        steps(patch, both)


def gather_first(serial, feats, coords, cells, patch):
    total, width = feats.shape
    vm = pl.BlockSpec(memory_space=pltpu.VMEM)
    hbm = pl.BlockSpec(memory_space=pltpu.HBM)
    picked = [jax.ShapeDtypeStruct((patch, width), F32), jax.ShapeDtypeStruct((patch, 128), F32)]
    return pl.pallas_call(
        first_kernel,
        in_specs=[hbm] * 4,
        out_specs=[vm] * 8,
        out_shape=[jax.ShapeDtypeStruct((patch + patch // 8, width), BF16)] * 2
        + [jax.ShapeDtypeStruct((total, width), F32), jax.ShapeDtypeStruct((total, 128), F32)]
        + picked * 2,
        scratch_shapes=[
            pltpu.SMEM((2 * patch,), jnp.int32),
            pltpu.VMEM(feats.shape, BF16),
            pltpu.VMEM(coords.shape, BF16),
            pltpu.VMEM(cells.shape, jnp.int32),
            pltpu.VMEM((8, total), F32),
            pltpu.SemaphoreType.DMA((4,)),
        ],
        compiler_params=pltpu.CompilerParams(vmem_limit_bytes=VMEM_LIMIT),
        name="gather_first",
    )(*[pltpu.with_memory_space_constraint(x, pltpu.HBM) for x in (serial, feats, coords, cells)])


def gather_second(serial, table, extra, picked, gain1, w_qkv, pos_proj):
    patch, width = picked[0].shape
    total = table.shape[0]
    vm = pl.BlockSpec(memory_space=pltpu.VMEM)
    return pl.pallas_call(
        second_kernel,
        in_specs=[pl.BlockSpec(memory_space=pltpu.SMEM)] + [vm] * 9,
        out_specs=[vm] * 6,
        out_shape=[jax.ShapeDtypeStruct((total, width), BF16)] * 5 + [jax.ShapeDtypeStruct((8, total), F32)],
        scratch_shapes=[pltpu.VMEM((2 * width, 4 * width), BF16)]
        + [pltpu.VMEM((patch, width), F32), pltpu.VMEM((patch, 128), F32)] * 3,
        compiler_params=pltpu.CompilerParams(vmem_limit_bytes=VMEM_LIMIT),
        name="gather_second",
    )(serial, table, extra, *picked, gain1, w_qkv, pos_proj)


def block_kernel(
    counts, ghosts, ordered, query, own_keys, own_values, side, cell_lines, face1, face2, face3, face4,
    gain1, w_qkv, pos_proj, w_out, gain2, w_up, w_down,
    out, pooled,
    w_full, keys, values, next_keys, next_values, faces, rows_all, sems,
):
    slot = pl.program_id(0)
    patch, width = out.shape
    slots = ghosts.shape[0]
    depth = width // HEADS
    sources = (face1, face2, face3, face4)

    @pl.when(slot == 0)
    def start():
        for j in range(slots):
            for g in range(4):
                @pl.when((j < counts[0]) & (ghosts[j] == g + 1))
                def fetch():
                    pltpu.make_async_copy(sources[g], faces.at[j], sems.at[j]).start()
        full_weights(w_full, w_qkv, pos_proj)
        values[:, width:] = jnp.ones((2 * patch, width), BF16)

    def arrive(slot_no):
        @pl.when((slot_no < counts[0]) & (ghosts[jnp.minimum(slot_no, slots - 1)] > 0))
        def wait():
            pltpu.make_async_copy(face1, faces.at[jnp.minimum(slot_no, slots - 1)], sems.at[jnp.minimum(slot_no, slots - 1)]).wait()

    def prepare(slot_no):
        ghost = ghosts[slot_no]
        slab_no = lax.axis_index("slab")
        sub_no = lax.axis_index("sub")
        on_x = ghost < 3
        down = (ghost == 1) | (ghost == 3)
        place = jnp.where(on_x, slab_no, sub_no)
        edge = jnp.where(down, 0, jnp.where(on_x, lax.axis_size("slab"), lax.axis_size("sub")) - 1)
        amount = jnp.where(place == edge, jnp.where(down, -1.0, 1.0), 0.0)
        bump = jnp.where(on_x, pos_proj[0:1, width:], pos_proj[1:2, width:]) * amount
        for lower in range(0, patch, CHUNK):
            there = normed_rows(faces[slot_no, lower : lower + CHUNK, :].astype(F32), gain1[...])
            yield
            first = patch + lower // 8
            line = jnp.concatenate(
                [faces[slot_no, first + c * 16 : first + c * 16 + 16, :] for c in range(CHUNK // 128)],
                axis=1,
            )
            both = dot(there, w_full[0:width, width:], ((1,), (0,)))
            lifted = dot(line, w_full[width : width + 16, width : 2 * width], ((0,), (0,)))
            next_keys[lower : lower + CHUNK, :] = (both[:, :width] + (lifted + bump)).astype(BF16)
            next_values[lower : lower + CHUNK, :] = both[:, width:].astype(BF16)
            yield

    @pl.when(slot == 0)
    def prime():
        arrive(0)
        for _ in prepare(0):
            pass

    live = slot < counts[0]
    base = pl.multiple_of(slot * patch, patch)

    @pl.when(jnp.logical_not(live))
    def dead():
        out[...] = jnp.zeros_like(out)
        rows_all[pl.ds(base, patch), :] = jnp.zeros((patch, 2 * width), BF16)

    def finish(lower, mixed):
        stream = (
            ordered[lower : lower + CHUNK, :].astype(F32) + dot(mixed.astype(BF16), w_out[...], ((1,), (0,)))
        ).astype(BF16)
        yield
        wide = stream.astype(F32)
        normed2 = normed_rows(wide, gain2[...])
        yield
        inner = jax.nn.gelu(dot(normed2, w_up[...], ((1,), (0,)))).astype(BF16)
        yield
        result = (wide + dot(inner, w_down[...], ((1,), (0,)))).astype(BF16)
        out[lower : lower + CHUNK, :] = result
        upper = side[lower : lower + CHUNK, :] > 0.5
        none = jnp.zeros_like(result)
        rows_all[pl.ds(base + lower, CHUNK), 0:width] = jnp.where(upper, none, result)
        rows_all[pl.ds(base + lower, CHUNK), width:] = jnp.where(upper, result, none)
        yield

    def attend(count):
        lane = lax.broadcasted_iota(jnp.int32, (CHUNK, width), 1)

        def head_scores(unit):
            lower = unit // HEADS * CHUNK
            h = unit % HEADS
            mine = (lane >= h * depth) & (lane < (h + 1) * depth)
            q = query[lower : lower + CHUNK, :]
            return mine, dot(jnp.where(mine, q, jnp.zeros_like(q)), keys[0:count, :], ((1,), (1,)))

        units = patch // CHUNK * HEADS
        tail = iter(())
        ahead_of = prepare(jnp.minimum(slot + 1, slots - 1))
        ahead = head_scores(0)
        mixed = jnp.zeros((CHUNK, width), F32)
        for unit in range(units):
            mine, scores = ahead
            if unit + 1 < units:
                ahead = head_scores(unit + 1)
            next(tail, None)
            if unit >= PREPARE_FROM:
                next(ahead_of, None)
            top = jnp.max(scores, axis=-1, keepdims=True)
            weights = jnp.exp2((scores - top) * SCALE).astype(BF16)
            summed = dot(weights, values[0:count, :], ((1,), (0,)))
            mixed = jnp.where(mine, summed[:, :width] / summed[:, width:], mixed)
            if unit % HEADS == HEADS - 1:
                tail = finish(unit // HEADS * CHUNK, mixed)
        for _ in tail:
            pass
        for _ in ahead_of:
            pass

    @pl.when(live)
    def work():
        keys[0:patch, :] = own_keys[...]
        values[0:patch, 0:width] = own_values[...]
        ghost = ghosts[slot]
        arrive(slot + 1)

        @pl.when(ghost > 0)
        def with_ghost():
            keys[patch:, :] = next_keys[...]
            values[patch:, 0:width] = next_values[...]
            attend(2 * patch)

        @pl.when(ghost == 0)
        def without_ghost():
            attend(patch)

    @pl.when(slot == slots - 1)
    def pool():
        half = pooled.shape[0] // 2
        row_no = lax.broadcasted_iota(jnp.int32, (1, slots * patch), 1)
        column = jnp.where(row_no < counts[0] * patch, cell_lines[0:1, :], -1.0)
        depth_no = cell_lines[1:2, :]
        ids = lax.broadcasted_iota(jnp.int32, (GRID, 1), 0).astype(F32)
        by_column = jnp.where(column == ids[0 : 2 * half // GRID], 1.0, 0.0).astype(BF16)
        by_depth = jnp.where(depth_no == ids, 1.0, 0.0).astype(BF16)
        tally = jnp.maximum(dot(by_depth, by_column, ((1,), (1,))), 1.0)
        lower_cell = (column - cell_lines[2:3, :] * (half // GRID)) * GRID + depth_no
        wide_ids = lax.broadcasted_iota(jnp.int32, (256, 1), 0).astype(F32)
        for c in range(half // 256):
            onehot = jnp.where(lower_cell == wide_ids + c * 256.0, 1.0, 0.0).astype(BF16)
            summed = dot(onehot, rows_all[...], ((1,), (0,)))
            for k in range(256 // GRID):
                part = summed[k * GRID : (k + 1) * GRID]
                for upper in range(2):
                    at = upper * (half // GRID) + c * (256 // GRID) + k
                    mean = part[:, upper * width : (upper + 1) * width] / tally[:, at : at + 1]
                    pooled[at * GRID : (at + 1) * GRID, :] = mean


def run_block(counts, ghosts, ordered, query, own_keys, own_values, side, cell_lines, faces, gain1, w_qkv, pos_proj, w_out, gain2, w_up, w_down, cells_total):
    slots = ghosts.shape[0]
    width = ordered.shape[1]
    patch = ordered.shape[0] // slots
    smem = pl.BlockSpec(memory_space=pltpu.SMEM)
    vm = pl.BlockSpec(memory_space=pltpu.VMEM)
    hbm = pl.BlockSpec(memory_space=pl.ANY)
    part = pl.BlockSpec((patch, width), lambda j: (j, 0))
    return pl.pallas_call(
        block_kernel,
        grid=(slots,),
        in_specs=[smem, smem] + [part] * 5 + [vm] + [hbm] * 4 + [vm] * 7,
        out_specs=[part, pl.BlockSpec((cells_total, width), lambda j: (0, 0))],
        out_shape=[
            jax.ShapeDtypeStruct((slots * patch, width), BF16),
            jax.ShapeDtypeStruct((cells_total, width), F32),
        ],
        scratch_shapes=[
            pltpu.VMEM((width + 16, 3 * width), BF16),
            pltpu.VMEM((2 * patch, width), BF16),
            pltpu.VMEM((2 * patch, 2 * width), BF16),
            pltpu.VMEM((patch, width), BF16),
            pltpu.VMEM((patch, width), BF16),
            pltpu.VMEM((slots,) + faces[0].shape, BF16),
            pltpu.VMEM((slots * patch, 2 * width), BF16),
            pltpu.SemaphoreType.DMA((slots,)),
        ],
        compiler_params=pltpu.CompilerParams(vmem_limit_bytes=VMEM_LIMIT),
        name="patch_block",
    )(counts, ghosts, ordered, query, own_keys, own_values, side, cell_lines, *faces, gain1, w_qkv, pos_proj, w_out, gain2, w_up, w_down)


def send(face, shift):
    received = []
    for axis in ("slab", "sub"):
        size = lax.axis_size(axis)
        received.append(lax.ppermute(face, axis, [(i, (i + shift) % size) for i in range(size)]))
    return received


def per_device(
    feats, coords, serial, cells, counts, ghosts, ln1_gain, w_qkv, pos_proj, w_out, ln2_gain, w_up, w_down
):
    rows_dev, width = feats.shape
    patch = rows_dev // ghosts.shape[0]
    slab_total = lax.axis_size("slab")
    sub_total = lax.axis_size("sub")
    cells2 = cells.reshape(1, rows_dev)
    gain1 = ln1_gain.reshape(1, width)
    face0, face1, table, extra, *picked = gather_first(serial, feats, coords, cells2, patch)
    own = gather_second(serial, table, extra, picked, gain1, w_qkv, pos_proj)
    below = send(face1, 1)
    above = send(face0, -1)
    faces = [below[0], above[0], below[1], above[1]]

    planes = GRID // slab_total
    lines = GRID // sub_total
    out, pooled = run_block(
        counts, ghosts, *own, faces,
        gain1, w_qkv, pos_proj, w_out, ln2_gain.reshape(1, width), w_up, w_down,
        planes * lines * GRID,
    )
    return out, pooled.reshape(planes, lines, GRID, width)


def solution(mesh):
    rows = P(("slab", "sub"))
    specs = (P(("slab", "sub"), None), P(None, ("slab", "sub")), rows, rows, rows, rows) + (P(),) * 7
    return jax.shard_map(
        per_device,
        mesh=mesh,
        in_specs=specs,
        out_specs=(P(("slab", "sub"), None), P("slab", "sub", None, None)),
        check_vma=False,
    )
```

```python
import functools
import math

import jax
import jax.numpy as jnp
from jax import lax
from jax.experimental import pallas as pl
from jax.experimental.pallas import tpu as pltpu
from jax.sharding import PartitionSpec as P

HEADS = 4
GRID = 64
EPS = 1e-05
CHUNK = 256
STEP = 1024
PREPARE_FROM = 0
SCALE = math.log2(math.e) / math.sqrt(32.0)
F32 = jnp.float32
BF16 = jnp.bfloat16
VMEM_LIMIT = 24 * 1024 * 1024


def dot(a, b, dims):
    return lax.dot_general(a, b, (dims, ((), ())), preferred_element_type=F32)


def normed_rows(values, gain):
    center = values - jnp.mean(values, axis=-1, keepdims=True)
    spread = jnp.mean(center * center, axis=-1, keepdims=True)
    return (center * lax.rsqrt(spread + EPS) * gain).astype(BF16)


def full_weights(w_full, w_qkv, pos_proj):
    width = w_qkv.shape[0]
    pos = pos_proj[...]
    high = pos.astype(BF16).astype(F32)
    rest = pos - high
    middle = rest.astype(BF16).astype(F32)
    low = rest - middle
    blank = jnp.zeros((16 - 9, 2 * width), F32)
    stacked = jnp.concatenate([high, middle, low, blank], axis=0).astype(BF16)
    w_full[0:width, 0 : 3 * width] = w_qkv[...]
    w_full[width : width + 16, 0 : 2 * width] = stacked
    w_full[width : width + 16, 2 * width : 3 * width] = jnp.zeros((16, width), BF16)
    if w_full.shape[0] > width + 16:
        w_full[width + 16 :, 0 : 3 * width] = jnp.zeros((width - 16, 3 * width), BF16)


def build_tables(feats, coords, cells, table, extra, lines):
    table[...] = feats[...].astype(F32)
    cell = cells[...]
    lines[0:3, :] = coords[...].astype(F32)
    lines[3:4, :] = (((cell >> 12) & 3) * 8 + ((cell >> 6) & 7)).astype(F32)
    lines[4:5, :] = (cell & 63).astype(F32)
    lines[5:6, :] = ((cell >> 13) & 1).astype(F32)
    lines[6:8, :] = jnp.zeros_like(lines[6:8, :])
    source = lax.broadcasted_iota(jnp.int32, (8, 128), 0)
    lane = lax.broadcasted_iota(jnp.int32, (8, 128), 1)
    place_spot = jnp.where((lane < 9) & (lane % 3 == source), 1.0, 0.0)
    cell_spot = jnp.where((lane == source + 6) & (source < 6), 1.0, 0.0)
    spot = jnp.where(source < 3, place_spot, cell_spot).astype(BF16)
    extra[...] = dot(lines[...].astype(BF16), spot, ((0,), (0,)))


def pick_rows(serial, first, base, table, extra, rows, more):
    for r in range(STEP):
        at = serial[first + base + r]
        rows[pl.ds(base + r, 1), :] = table[pl.ds(at, 1), :]
        more[pl.ds(base + r, 1), :] = extra[pl.ds(at, 1), :]


def make_face(face, rows, more):
    patch = rows.shape[0]
    row = lax.broadcasted_iota(jnp.int32, (16, 128), 0)
    lane = lax.broadcasted_iota(jnp.int32, (16, 128), 1)
    pick = jnp.where((row == lane) & (row < 9), 1.0, 0.0).astype(BF16)
    face[0:patch, :] = rows[...].astype(BF16)
    line = dot(pick, more[...].astype(BF16), ((1,), (1,))).astype(BF16)
    for c in range(patch // 128):
        face[patch + c * 16 : patch + c * 16 + 16, :] = line[:, c * 128 : c * 128 + 128]


def project_weights(w_full, w_qkv, pos_proj):
    width = w_qkv.shape[0]
    full_weights(w_full, w_qkv, pos_proj)
    row = lax.broadcasted_iota(jnp.int32, (width, width), 0)
    w_full[0:width, 3 * width :] = jnp.zeros((width, width), BF16)
    w_full[width:, 3 * width :] = jnp.where(row == 11, 1.0, 0.0).astype(BF16)


def project(base, offset, rows, more, gain1, w_full, outs):
    ordered, query, keys, values, side, cell_lines = outs
    width = rows.shape[1]
    row = lax.broadcasted_iota(jnp.int32, (8, 128), 0)
    lane = lax.broadcasted_iota(jnp.int32, (8, 128), 1)
    pick = jnp.where((row < 3) & (lane == row + 9), 1.0, 0.0).astype(BF16)
    wide = rows[pl.ds(base, STEP), :]
    aux = more[pl.ds(base, STEP), :].astype(BF16)
    normed = normed_rows(wide, gain1[...])
    qkv = dot(jnp.concatenate([normed, aux], axis=1), w_full[...], ((1,), (0,)))
    span = pl.ds(pl.multiple_of(base + offset, STEP), STEP)
    ordered[span, :] = wide.astype(BF16)
    query[span, :] = qkv[:, :width].astype(BF16)
    keys[span, :] = qkv[:, width : 2 * width].astype(BF16)
    values[span, :] = qkv[:, 2 * width : 3 * width].astype(BF16)
    side[span, :] = qkv[:, 3 * width :].astype(BF16)
    cell_lines[:, span] = dot(pick, aux, ((1,), (1,)))


def steps(patch, body):
    def step(block, carry):
        body(pl.multiple_of(block * STEP, STEP))
        return carry

    lax.fori_loop(0, patch // STEP, step, 0)


def first_kernel(
    serial_in, feats_in, coords_in, cells_in,
    face0, face1, table, extra, rows0, more0, rows1, more1,
    serial, feats, coords, cells, lines, sems,
):
    patch = rows1.shape[0]
    copies = [
        pltpu.make_async_copy(feats_in, feats, sems.at[0]),
        pltpu.make_async_copy(coords_in, coords, sems.at[1]),
        pltpu.make_async_copy(cells_in, cells, sems.at[2]),
        pltpu.make_async_copy(serial_in.at[pl.ds(0, 2 * patch)], serial, sems.at[3]),
    ]
    for copy in copies:
        copy.start()
    for copy in copies:
        copy.wait()
    build_tables(feats, coords, cells, table, extra, lines)
    steps(patch, lambda base: pick_rows(serial, 0, base, table, extra, rows0, more0))
    make_face(face0, rows0, more0)
    steps(patch, lambda base: pick_rows(serial, patch, base, table, extra, rows1, more1))
    make_face(face1, rows1, more1)


def second_kernel(
    serial, table, extra, rows0, more0, rows1, more1, gain1, w_qkv, pos_proj,
    ordered, query, keys, values, side, cell_lines,
    w_full, rows2, more2, rows3, more3, rows4, more4,
):
    patch = rows1.shape[0]
    outs = (ordered, query, keys, values, side, cell_lines)
    picked = ((rows0, more0), (rows1, more1), (rows2, more2), (rows3, more3), (rows4, more4))
    project_weights(w_full, w_qkv, pos_proj)
    for slot in range(len(picked)):
        def both(base):
            if slot + 2 < len(picked):
                pick_rows(serial, (slot + 2) * patch, base, table, extra, *picked[slot + 2])
            project(base, slot * patch, *picked[slot], gain1, w_full, outs)

        steps(patch, both)


def gather_first(serial, feats, coords, cells, patch):
    total, width = feats.shape
    vm = pl.BlockSpec(memory_space=pltpu.VMEM)
    hbm = pl.BlockSpec(memory_space=pltpu.HBM)
    picked = [jax.ShapeDtypeStruct((patch, width), F32), jax.ShapeDtypeStruct((patch, 128), F32)]
    return pl.pallas_call(
        first_kernel,
        in_specs=[hbm] * 4,
        out_specs=[vm] * 8,
        out_shape=[jax.ShapeDtypeStruct((patch + patch // 8, width), BF16)] * 2
        + [jax.ShapeDtypeStruct((total, width), F32), jax.ShapeDtypeStruct((total, 128), F32)]
        + picked * 2,
        scratch_shapes=[
            pltpu.SMEM((2 * patch,), jnp.int32),
            pltpu.VMEM(feats.shape, BF16),
            pltpu.VMEM(coords.shape, BF16),
            pltpu.VMEM(cells.shape, jnp.int32),
            pltpu.VMEM((8, total), F32),
            pltpu.SemaphoreType.DMA((4,)),
        ],
        compiler_params=pltpu.CompilerParams(vmem_limit_bytes=VMEM_LIMIT),
        name="gather_first",
    )(*[pltpu.with_memory_space_constraint(x, pltpu.HBM) for x in (serial, feats, coords, cells)])


def gather_second(serial, table, extra, picked, gain1, w_qkv, pos_proj):
    patch, width = picked[0].shape
    total = table.shape[0]
    vm = pl.BlockSpec(memory_space=pltpu.VMEM)
    return pl.pallas_call(
        second_kernel,
        in_specs=[pl.BlockSpec(memory_space=pltpu.SMEM)] + [vm] * 9,
        out_specs=[vm] * 6,
        out_shape=[jax.ShapeDtypeStruct((total, width), BF16)] * 5 + [jax.ShapeDtypeStruct((8, total), F32)],
        scratch_shapes=[pltpu.VMEM((2 * width, 4 * width), BF16)]
        + [pltpu.VMEM((patch, width), F32), pltpu.VMEM((patch, 128), F32)] * 3,
        compiler_params=pltpu.CompilerParams(vmem_limit_bytes=VMEM_LIMIT),
        name="gather_second",
    )(serial, table, extra, *picked, gain1, w_qkv, pos_proj)


def block_kernel(
    counts, ghosts, ordered, query, own_keys, own_values, side, cell_lines, face1, face2, face3, face4,
    gain1, w_qkv, pos_proj, w_out, gain2, w_up, w_down,
    out, pooled,
    w_full, keys, values, next_keys, next_values, faces, rows_all, sems,
):
    slot = pl.program_id(0)
    patch, width = out.shape
    slots = ghosts.shape[0]
    depth = width // HEADS
    sources = (face3, face4, face1, face2)

    @pl.when(slot == 0)
    def start():
        for j in range(slots):
            for g in range(4):
                @pl.when((j < counts[0]) & (ghosts[j] == g + 1))
                def fetch():
                    pltpu.make_async_copy(sources[g], faces.at[j], sems.at[j]).start()
        full_weights(w_full, w_qkv, pos_proj)
        values[:, width:] = jnp.ones((2 * patch, width), BF16)

    def arrive(slot_no):
        @pl.when((slot_no < counts[0]) & (ghosts[jnp.minimum(slot_no, slots - 1)] > 0))
        def wait():
            pltpu.make_async_copy(face1, faces.at[jnp.minimum(slot_no, slots - 1)], sems.at[jnp.minimum(slot_no, slots - 1)]).wait()

    def prepare(slot_no):
        ghost = ghosts[slot_no]
        slab_no = lax.axis_index("slab")
        sub_no = lax.axis_index("sub")
        on_x = ghost < 3
        down = (ghost == 1) | (ghost == 3)
        place = jnp.where(on_x, slab_no, sub_no)
        edge = jnp.where(down, 0, jnp.where(on_x, lax.axis_size("slab"), lax.axis_size("sub")) - 1)
        amount = jnp.where(place == edge, jnp.where(down, -1.0, 1.0), 0.0)
        bump = jnp.where(on_x, pos_proj[0:1, width:], pos_proj[1:2, width:]) * amount
        for lower in range(0, patch, CHUNK):
            there = normed_rows(faces[slot_no, lower : lower + CHUNK, :].astype(F32), gain1[...])
            yield
            first = patch + lower // 8
            line = jnp.concatenate(
                [faces[slot_no, first + c * 16 : first + c * 16 + 16, :] for c in range(CHUNK // 128)],
                axis=1,
            )
            both = dot(there, w_full[0:width, width:], ((1,), (0,)))
            lifted = dot(line, w_full[width : width + 16, width : 2 * width], ((0,), (0,)))
            next_keys[lower : lower + CHUNK, :] = (both[:, :width] + (lifted + bump)).astype(BF16)
            next_values[lower : lower + CHUNK, :] = both[:, width:].astype(BF16)
            yield

    @pl.when(slot == 0)
    def prime():
        arrive(0)
        for _ in prepare(0):
            pass

    live = slot < counts[0]
    base = pl.multiple_of(slot * patch, patch)

    @pl.when(jnp.logical_not(live))
    def dead():
        out[...] = jnp.zeros_like(out)
        rows_all[pl.ds(base, patch), :] = jnp.zeros((patch, 2 * width), BF16)

    def finish(lower, mixed):
        stream = (
            ordered[lower : lower + CHUNK, :].astype(F32) + dot(mixed.astype(BF16), w_out[...], ((1,), (0,)))
        ).astype(BF16)
        yield
        wide = stream.astype(F32)
        normed2 = normed_rows(wide, gain2[...])
        yield
        inner = jax.nn.gelu(dot(normed2, w_up[...], ((1,), (0,)))).astype(BF16)
        yield
        result = (wide + dot(inner, w_down[...], ((1,), (0,)))).astype(BF16)
        out[lower : lower + CHUNK, :] = result
        upper = side[lower : lower + CHUNK, :] > 0.5
        none = jnp.zeros_like(result)
        rows_all[pl.ds(base + lower, CHUNK), 0:width] = jnp.where(upper, none, result)
        rows_all[pl.ds(base + lower, CHUNK), width:] = jnp.where(upper, result, none)
        yield

    def attend(count):
        lane = lax.broadcasted_iota(jnp.int32, (CHUNK, width), 1)

        def head_scores(unit):
            lower = unit // HEADS * CHUNK
            h = unit % HEADS
            mine = (lane >= h * depth) & (lane < (h + 1) * depth)
            q = query[lower : lower + CHUNK, :]
            return mine, dot(jnp.where(mine, q, jnp.zeros_like(q)), keys[0:count, :], ((1,), (1,)))

        units = patch // CHUNK * HEADS
        tail = iter(())
        ahead_of = prepare(jnp.minimum(slot + 1, slots - 1))
        ahead = head_scores(0)
        mixed = jnp.zeros((CHUNK, width), F32)
        for unit in range(units):
            mine, scores = ahead
            if unit + 1 < units:
                ahead = head_scores(unit + 1)
            next(tail, None)
            if unit >= PREPARE_FROM:
                next(ahead_of, None)
            top = jnp.max(scores, axis=-1, keepdims=True)
            weights = jnp.exp2((scores - top) * SCALE).astype(BF16)
            summed = dot(weights, values[0:count, :], ((1,), (0,)))
            mixed = jnp.where(mine, summed[:, :width] / summed[:, width:], mixed)
            if unit % HEADS == HEADS - 1:
                tail = finish(unit // HEADS * CHUNK, mixed)
        for _ in tail:
            pass
        for _ in ahead_of:
            pass

    @pl.when(live)
    def work():
        keys[0:patch, :] = own_keys[...]
        values[0:patch, 0:width] = own_values[...]
        ghost = ghosts[slot]
        arrive(slot + 1)

        @pl.when(ghost > 0)
        def with_ghost():
            keys[patch:, :] = next_keys[...]
            values[patch:, 0:width] = next_values[...]
            attend(2 * patch)

        @pl.when(ghost == 0)
        def without_ghost():
            attend(patch)

    @pl.when(slot == slots - 1)
    def pool():
        half = pooled.shape[0] // 2
        row_no = lax.broadcasted_iota(jnp.int32, (1, slots * patch), 1)
        column = jnp.where(row_no < counts[0] * patch, cell_lines[0:1, :], -1.0)
        depth_no = cell_lines[1:2, :]
        ids = lax.broadcasted_iota(jnp.int32, (GRID, 1), 0).astype(F32)
        by_column = jnp.where(column == ids[0 : 2 * half // GRID], 1.0, 0.0).astype(BF16)
        by_depth = jnp.where(depth_no == ids, 1.0, 0.0).astype(BF16)
        tally = jnp.maximum(dot(by_depth, by_column, ((1,), (1,))), 1.0)
        lower_cell = (column - cell_lines[2:3, :] * (half // GRID)) * GRID + depth_no
        wide_ids = lax.broadcasted_iota(jnp.int32, (256, 1), 0).astype(F32)
        for c in range(half // 256):
            onehot = jnp.where(lower_cell == wide_ids + c * 256.0, 1.0, 0.0).astype(BF16)
            summed = dot(onehot, rows_all[...], ((1,), (0,)))
            for k in range(256 // GRID):
                part = summed[k * GRID : (k + 1) * GRID]
                for upper in range(2):
                    at = upper * (half // GRID) + c * (256 // GRID) + k
                    mean = part[:, upper * width : (upper + 1) * width] / tally[:, at : at + 1]
                    pooled[at * GRID : (at + 1) * GRID, :] = mean


def run_block(counts, ghosts, ordered, query, own_keys, own_values, side, cell_lines, faces, gain1, w_qkv, pos_proj, w_out, gain2, w_up, w_down, cells_total):
    slots = ghosts.shape[0]
    width = ordered.shape[1]
    patch = ordered.shape[0] // slots
    smem = pl.BlockSpec(memory_space=pltpu.SMEM)
    vm = pl.BlockSpec(memory_space=pltpu.VMEM)
    hbm = pl.BlockSpec(memory_space=pl.ANY)
    part = pl.BlockSpec((patch, width), lambda j: (j, 0))
    return pl.pallas_call(
        block_kernel,
        grid=(slots,),
        in_specs=[smem, smem] + [part] * 5 + [vm] + [hbm] * 4 + [vm] * 7,
        out_specs=[part, pl.BlockSpec((cells_total, width), lambda j: (0, 0))],
        out_shape=[
            jax.ShapeDtypeStruct((slots * patch, width), BF16),
            jax.ShapeDtypeStruct((cells_total, width), F32),
        ],
        scratch_shapes=[
            pltpu.VMEM((width + 16, 3 * width), BF16),
            pltpu.VMEM((2 * patch, width), BF16),
            pltpu.VMEM((2 * patch, 2 * width), BF16),
            pltpu.VMEM((patch, width), BF16),
            pltpu.VMEM((patch, width), BF16),
            pltpu.VMEM((slots,) + faces[0].shape, BF16),
            pltpu.VMEM((slots * patch, 2 * width), BF16),
            pltpu.SemaphoreType.DMA((slots,)),
        ],
        compiler_params=pltpu.CompilerParams(vmem_limit_bytes=VMEM_LIMIT),
        name="patch_block",
    )(counts, ghosts, ordered, query, own_keys, own_values, side, cell_lines, *faces, gain1, w_qkv, pos_proj, w_out, gain2, w_up, w_down)


def send(face, shift):
    received = []
    for axis in ("sub", "slab"):
        size = lax.axis_size(axis)
        received.append(lax.ppermute(face, axis, [(i, (i + shift) % size) for i in range(size)]))
    return received


def per_device(
    feats, coords, serial, cells, counts, ghosts, ln1_gain, w_qkv, pos_proj, w_out, ln2_gain, w_up, w_down
):
    rows_dev, width = feats.shape
    patch = rows_dev // ghosts.shape[0]
    slab_total = lax.axis_size("slab")
    sub_total = lax.axis_size("sub")
    cells2 = cells.reshape(1, rows_dev)
    gain1 = ln1_gain.reshape(1, width)
    face0, face1, table, extra, *picked = gather_first(serial, feats, coords, cells2, patch)
    own = gather_second(serial, table, extra, picked, gain1, w_qkv, pos_proj)
    below = send(face1, 1)
    above = send(face0, -1)
    faces = [below[0], above[0], below[1], above[1]]

    planes = GRID // slab_total
    lines = GRID // sub_total
    out, pooled = run_block(
        counts, ghosts, *own, faces,
        gain1, w_qkv, pos_proj, w_out, ln2_gain.reshape(1, width), w_up, w_down,
        planes * lines * GRID,
    )
    return out, pooled.reshape(planes, lines, GRID, width)


def solution(mesh):
    rows = P(("slab", "sub"))
    specs = (P(("slab", "sub"), None), P(None, ("slab", "sub")), rows, rows, rows, rows) + (P(),) * 7
    return jax.shard_map(
        per_device,
        mesh=mesh,
        in_specs=specs,
        out_specs=(P(("slab", "sub"), None), P("slab", "sub", None, None)),
        check_vma=False,
    )
```
